32 devices in a mesh: dp: 8 (over y, x, core), tensor: 4 (over z).
Axes of the slice: x: 2, y: 2, z: 4, core: 2. Of those that a mesh axis runs over, the one named last changes fastest.
Arguments:
- hidden_in: bfloat16 [8192, 768], P(('dp', 'tensor')), may hold values from -40 to 40
- segment_ids: int32 [16, 512], P('dp'), may hold values from 0 to 7, never falling along the last dimension, each value on 1 to 256 neighbouring positions
- cotangent: float32 [8192, 768], P(('dp', 'tensor')), may hold values from -6 to 6
- norm1_gain: float32 [768], P(('dp', 'tensor')), may hold values from 0.5 to 1.5
- norm1_bias: float32 [768], P(('dp', 'tensor')), may hold values from -2 to 2
- norm2_gain: float32 [768], P(('dp', 'tensor')), may hold values from 0.5 to 1.5
- norm2_bias: float32 [768], P(('dp', 'tensor')), may hold values from -2 to 2
- qkv_weight: bfloat16 [768, 2304], P('dp', 'tensor'), may hold values from -2 to 2
- qkv_bias: bfloat16 [12, 192], P('tensor', 'dp'), may hold values from -3 to 3
- dense_weight: bfloat16 [768, 768], P('tensor', 'dp'), may hold values from -0.875 to 0.875
- dense_bias: float32 [768], P(('dp', 'tensor')), may hold values from -3 to 3
- up_weight: bfloat16 [768, 3072], P('dp', 'tensor'), may hold values from -0.21875 to 0.21875
- up_bias: bfloat16 [12, 256], P('tensor', 'dp'), may hold values from -3 to 3
- down_weight: bfloat16 [3072, 768], P('tensor', 'dp'), may hold values from -0.109375 to 0.109375
- down_bias: float32 [768], P(('dp', 'tensor')), may hold values from -3 to 3
Outputs:
- hidden_out: float32 [8192, 768], P(('dp', 'tensor'))
- hidden_grad: float32 [8192, 768], P(('dp', 'tensor'))
- norm1_gain_grad: float32 [768], P(('dp', 'tensor'))
- norm1_bias_grad: float32 [768], P(('dp', 'tensor'))
- norm2_gain_grad: float32 [768], P(('dp', 'tensor'))
- norm2_bias_grad: float32 [768], P(('dp', 'tensor'))
- qkv_weight_grad: float32 [768, 2304], P('dp', 'tensor')
- qkv_bias_grad: float32 [12, 192], P('tensor', 'dp')
- dense_weight_grad: float32 [768, 768], P('tensor', 'dp')
- dense_bias_grad: float32 [768], P(('dp', 'tensor'))
- up_weight_grad: float32 [768, 3072], P('dp', 'tensor')
- up_bias_grad: float32 [12, 256], P('tensor', 'dp')
- down_weight_grad: float32 [3072, 768], P('tensor', 'dp')
- down_bias_grad: float32 [768], P(('dp', 'tensor'))
The draws below stay inside these ranges and needn't reach their ends.
Inputs may be any that keep to these rules, and one draw needn't show every extreme that they name: `segment_ids`: within each row of 512 tokens the ids never fall; each document holds 1 to 256 tokens, and some document holds exactly 256.
All inputs are finite; a program needn't handle non-finite values.
Results may differ from the reference program's by a relative error of at most 0.0082.
Values may be sent and summed in bfloat16 or wider, within the bound.
No kernel may reach another device: no remote copies, remote signals or barrier semaphores. Data moves between devices by JAX's collectives and lax.ppermute only.
A program may use at most 128 MiB of HBM per device.

```python
import math
import jax
import jax.numpy as jnp
import numpy as np
from jax import lax

D = 768
HEADS = 12
HD = 64
ROT = 16
FF = 3072
LEN = 512
DOCS = 8
BIAS_ROW = 256
SEQS = 16
TOKENS = 8192


def draw_hidden_in(key, part):
    first_key, second_key, third_key = jax.random.split(key, 3)
    base = jnp.clip(jax.random.normal(first_key, (TOKENS, D), jnp.float32), -4.0, 4.0)
    row_scale = jnp.exp(jax.random.uniform(second_key, (TOKENS, 1), jnp.float32, math.log(0.3), math.log(3.0)))
    column_scale = jnp.exp(jax.random.uniform(third_key, (1, D), jnp.float32, 0.0, math.log(3.0)))
    return (base * row_scale * column_scale).astype(jnp.bfloat16)


def draw_qkv_weight(key, part):
    first_key = jax.random.fold_in(key, 0)
    base = jnp.clip(jax.random.normal(first_key, (D, HEADS, 3, HD), jnp.float32), -4.0, 4.0) * D ** (-0.5)
    return base.reshape(D, 3 * D).astype(jnp.bfloat16)


def with_spikes(array, rng, source, target, blocks, factor):
    def block_of(axis_at):
        return (jnp.arange(array.shape[axis_at]) // (array.shape[axis_at] // blocks)).reshape((-1,) + (1,) * (array.ndim - 1 - axis_at))

    near = jax.random.permutation(rng, blocks)[block_of(target)]
    far = (block_of(target) + blocks // 2) % blocks
    return jnp.where((block_of(source) == near) | (block_of(source) == far), factor * array, array)


def steps_of(stream_key, extent, pieces, smallest, high):
    level = 1.0
    for axis_at, parts in pieces:
        heights = jax.random.uniform(jax.random.fold_in(jax.random.fold_in(stream_key, 6), axis_at), (parts,), jnp.float32, smallest / len(pieces), high / len(pieces))
        level = level * jnp.repeat(jnp.exp(heights), extent[axis_at] // parts).reshape((-1,) + (1,) * (len(extent) - 1 - axis_at))
    return level


def profile(amount, total, most, skew):
    loads = [(1 << 20) // math.isqrt(grade ** skew) + 1 for grade in range(2, amount + 1)]
    spare, given = total - most - (amount - 1), [1] * (amount - 1)
    while spare > 0:
        candidates = [i for i in range(amount - 1) if given[i] < most]
        mass, remaining = sum([loads[i] for i in candidates]), spare
        for i in candidates:
            addition = min(most - given[i], max(1, remaining * loads[i] // mass), spare)
            given[i] = given[i] + addition
            spare = spare - addition
    return np.array([most] + given)


def uneven(stream_key, number_of, total, most, slope):
    if number_of == 2:
        one = jax.random.randint(stream_key, (), max(1, total - most), min(most, total - 1) + 1)
        return jnp.stack([one, total - one])
    tallies = jnp.asarray(profile(number_of, total, most, slope), jnp.int32)
    twos = (number_of - 1) // 2
    giver, receiver = tallies[1:1 + 2 * twos:2], tallies[2:2 + 2 * twos:2]
    room = jnp.minimum(giver - 1, most - receiver)
    shifted = jax.random.randint(jax.random.fold_in(stream_key, 1), (twos,), 0, 1 << 20) % (room + 1)
    tallies = tallies.at[1:1 + 2 * twos:2].set(giver - shifted).at[2:2 + 2 * twos:2].set(receiver + shifted)
    return tallies[jax.random.permutation(jax.random.fold_in(stream_key, 2), number_of)]


def scatter_about(key, shape, deviation, reach, cuts=(), dtype=jnp.bfloat16):
    values = deviation * jax.random.normal(key, shape, jnp.float32)
    if cuts:
        values = values * steps_of(key, shape, cuts, -0.22, 0.18)
    return jnp.clip(values, -reach, reach).astype(dtype)


def heavy_noise(own_key, shape, scale, most, shards, heavy, held_as=jnp.bfloat16):
    values = scale * jax.random.normal(own_key, shape, jnp.float32)
    if shards:
        values = values * steps_of(own_key, shape, shards, -0.22, 0.18)
    return jnp.clip(with_spikes(values, jax.random.fold_in(own_key, 3), *heavy), -most, most).astype(held_as)


def setup_inputs(seed: int = 0) -> dict:
    key_list = jax.random.split(jax.random.key(seed), 16)
    hidden_in = draw_hidden_in(jax.random.fold_in(key_list[15], 71), 0)
    segment_ids = jax.vmap(lambda own: jnp.searchsorted(jnp.cumsum(uneven(own, DOCS, LEN, LEN // 2, 2)), jnp.arange(LEN), side="right"))(jax.random.split(key_list[1], SEQS)).reshape((SEQS, LEN)).astype(jnp.int32)
    cotangent = heavy_noise(key_list[2], (TOKENS, D), 1.0, 6.0, ((0, 32),), (0, 1, 32, 2.75), jnp.float32)
    norm1_gain = jnp.clip(1.0 + 0.1 * jax.random.normal(key_list[3], (D,), jnp.float32), 0.5, 1.5)
    norm1_bias = scatter_about(key_list[4], (D,), 0.3, 2.0, ((0, 32),), jnp.float32)
    norm2_gain = jnp.clip(1.0 + 0.1 * jax.random.normal(key_list[5], (D,), jnp.float32), 0.5, 1.5)
    norm2_bias = scatter_about(key_list[6], (D,), 0.3, 2.0, ((0, 32),), jnp.float32)
    qkv_weight = draw_qkv_weight(jax.random.fold_in(key_list[15], 71), 0)
    qkv_bias = scatter_about(key_list[8], (HEADS, 3 * HD), 0.5, 3.0, ((0, 4), (1, 8)))
    dense_weight = scatter_about(key_list[9], (D, D), (D // 16) ** -0.5, 0.875, ((0, 4), (1, 8)))
    dense_bias = scatter_about(key_list[10], (D,), 0.5, 3.0, ((0, 32),), jnp.float32)
    up_weight = scatter_about(key_list[11], (D, FF), D ** -0.5, 0.21875, ((0, 8), (1, 4)))
    up_bias = scatter_about(key_list[12], (FF // BIAS_ROW, BIAS_ROW), 0.5, 3.0, ((0, 4), (1, 8)))
    down_weight = scatter_about(key_list[13], (FF, D), FF ** -0.5, 0.109375, ((0, 4), (1, 8)))
    down_bias = scatter_about(key_list[14], (D,), 0.5, 3.0, ((0, 32),), jnp.float32)
    return dict(hidden_in=hidden_in, segment_ids=segment_ids, cotangent=cotangent, norm1_gain=norm1_gain, norm1_bias=norm1_bias, norm2_gain=norm2_gain, norm2_bias=norm2_bias, qkv_weight=qkv_weight, qkv_bias=qkv_bias, dense_weight=dense_weight, dense_bias=dense_bias, up_weight=up_weight, up_bias=up_bias, down_weight=down_weight, down_bias=down_bias)


norm_eps = 1e-05

def rotary_tables(length, rot_dims):
    places = jnp.arange(length).astype(jnp.float32)
    frequency = 1.0 / 10000.0 ** (jnp.arange(0, rot_dims, 2).astype(jnp.float32) / rot_dims)
    angles = places[:, None] * frequency[None, :]
    angles = jnp.concatenate([angles, angles], axis=1)
    return (jnp.cos(angles)[:, None, :], jnp.sin(angles)[:, None, :])

def rotate_apply(entries, cosine, sine, rot_dims):
    half_dims = rot_dims // 2
    front = entries[..., :rot_dims]
    turned = jnp.concatenate([-front[..., half_dims:], front[..., :half_dims]], axis=-1)
    return jnp.concatenate([front * cosine + turned * sine, entries[..., rot_dims:]], axis=-1)

def rotate_back(grads, cosine, sine, rot_dims):
    half_dims = rot_dims // 2
    front = grads[..., :rot_dims]
    scaled = front * sine
    turned = jnp.concatenate([scaled[..., half_dims:], -scaled[..., :half_dims]], axis=-1)
    return jnp.concatenate([front * cosine + turned, grads[..., rot_dims:]], axis=-1)

def normalize(wide_rows):
    centre = lax.optimization_barrier(jnp.mean(wide_rows, axis=-1, keepdims=True))
    spread = lax.optimization_barrier(jnp.mean(jnp.square(wide_rows - centre), axis=-1, keepdims=True))
    inverse = lax.rsqrt(spread + norm_eps)
    return ((wide_rows - centre) * inverse, inverse)

def gelu_exact(values):
    return 0.5 * values * (1.0 + lax.erf(values * (1.0 / math.sqrt(2.0))))

def gelu_slope(values):
    cumulative = 0.5 * (1.0 + lax.erf(values * (1.0 / math.sqrt(2.0))))
    density = jnp.exp(-0.5 * values * values) * (1.0 / math.sqrt(2.0 * math.pi))
    return cumulative + values * density

def allowed_pairs(segment):
    length = segment.shape[-1]
    earlier = lax.broadcasted_iota(jnp.int32, (length, length), 0) >= lax.broadcasted_iota(jnp.int32, (length, length), 1)
    return (segment[:, :, None] == segment[:, None, :]) & earlier[None]

def attend_scores(queries, key_rows, segment):
    scaling = queries.shape[-1] ** (-0.5)
    scores = jnp.einsum('bqhd,bkhd->bhqk', queries.astype(jnp.float32), key_rows.astype(jnp.float32)) * scaling
    return jnp.where(allowed_pairs(segment)[:, None], scores, -1e+30)

def attend_forward(queries, key_rows, value_rows, segment):
    scores = attend_scores(queries, key_rows, segment)
    highest = lax.optimization_barrier(jnp.max(scores, axis=-1, keepdims=True))
    logsum = highest + jnp.log(lax.optimization_barrier(jnp.sum(jnp.exp(scores - highest), axis=-1, keepdims=True)))
    weights = jnp.exp(scores - logsum).astype(jnp.bfloat16)
    output = jnp.einsum('bhqk,bkhd->bqhd', weights.astype(jnp.float32), value_rows.astype(jnp.float32))
    return (output.astype(jnp.bfloat16), logsum)

def attend_backward(queries, key_rows, value_rows, segment, logsum, grad_out):
    scaling = queries.shape[-1] ** (-0.5)
    scores = attend_scores(queries, key_rows, segment)
    weights = jnp.exp(scores - logsum)
    weights_half = weights.astype(jnp.bfloat16)
    grad_weights = jnp.einsum('bqhd,bkhd->bhqk', grad_out.astype(jnp.float32), value_rows.astype(jnp.float32))
    inner_sum = lax.optimization_barrier(jnp.sum(weights * grad_weights, axis=-1, keepdims=True))
    grad_scores = (weights * (grad_weights - inner_sum) * scaling).astype(jnp.bfloat16)
    grad_queries = jnp.einsum('bhqk,bkhd->bqhd', grad_scores.astype(jnp.float32), key_rows.astype(jnp.float32))
    grad_keys = jnp.einsum('bhqk,bqhd->bkhd', grad_scores.astype(jnp.float32), queries.astype(jnp.float32))
    grad_values = jnp.einsum('bhqk,bqhd->bkhd', weights_half.astype(jnp.float32), grad_out.astype(jnp.float32))
    return (grad_queries, grad_keys, grad_values)

def rows_product(left, right):
    return jnp.dot(left.T, right, preferred_element_type=jnp.float32)

def cols_product(left, right):
    return jnp.dot(left, right.T, preferred_element_type=jnp.float32)

def reference(hidden_in, segment_ids, cotangent, norm1_gain, norm1_bias, norm2_gain, norm2_bias, qkv_weight, qkv_bias, dense_weight, dense_bias, up_weight, up_bias, down_weight, down_bias):
    cosine, sine = rotary_tables(LEN, ROT)
    qkv_shift = qkv_bias.reshape(-1).astype(jnp.float32)
    up_shift = up_bias.reshape(-1).astype(jnp.float32)

    def one_sequence(totals, inputs):
        rows_in, cot_rows, segment = inputs
        wide_rows = rows_in.astype(jnp.float32)
        normed, inverse = normalize(wide_rows)
        first = (normed * norm1_gain + norm1_bias).astype(jnp.bfloat16)
        second = (normed * norm2_gain + norm2_bias).astype(jnp.bfloat16)
        mixed = (jnp.dot(first, qkv_weight, preferred_element_type=jnp.float32) + qkv_shift).reshape(LEN, HEADS, 3, HD)
        queries = rotate_apply(mixed[:, :, 0], cosine, sine, ROT).astype(jnp.bfloat16)[None]
        key_rows = rotate_apply(mixed[:, :, 1], cosine, sine, ROT).astype(jnp.bfloat16)[None]
        value_rows = mixed[:, :, 2].astype(jnp.bfloat16)[None]
        attended, logsum = attend_forward(queries, key_rows, value_rows, segment[None])
        attended_flat = attended[0].reshape(LEN, D)
        inner_pre = jnp.dot(second, up_weight, preferred_element_type=jnp.float32) + up_shift
        active = gelu_exact(inner_pre).astype(jnp.bfloat16)
        branch = jnp.dot(attended_flat, dense_weight, preferred_element_type=jnp.float32) + jnp.dot(active, down_weight, preferred_element_type=jnp.float32)
        result = wide_rows + branch + dense_bias + down_bias
        cot_half = cot_rows.astype(jnp.bfloat16)
        grad_down = rows_product(active, cot_half)
        grad_active = cols_product(cot_half, down_weight)
        grad_pre = grad_active * gelu_slope(inner_pre)
        grad_pre_half = grad_pre.astype(jnp.bfloat16)
        grad_up = rows_product(second, grad_pre_half)
        grad_second = cols_product(grad_pre_half, up_weight)
        grad_dense = rows_product(attended_flat, cot_half)
        grad_attended = cols_product(cot_half, dense_weight).astype(jnp.bfloat16).reshape(1, LEN, HEADS, HD)
        grad_queries, grad_keys, grad_values = attend_backward(queries, key_rows, value_rows, segment[None], logsum, grad_attended)
        grad_mixed = jnp.stack([rotate_back(grad_queries[0], cosine, sine, ROT), rotate_back(grad_keys[0], cosine, sine, ROT), grad_values[0]], axis=2).reshape(LEN, 3 * D)
        grad_mixed_half = grad_mixed.astype(jnp.bfloat16)
        grad_qkv = rows_product(first, grad_mixed_half)
        grad_first = cols_product(grad_mixed_half, qkv_weight)
        grad_normed = grad_first * norm1_gain + grad_second * norm2_gain
        grad_rows = inverse * (grad_normed - lax.optimization_barrier(jnp.mean(grad_normed, axis=-1, keepdims=True)) - normed * lax.optimization_barrier(jnp.mean(grad_normed * normed, axis=-1, keepdims=True)))
        input_grad = cot_rows + grad_rows
        terms = (lax.optimization_barrier(jnp.sum(grad_first * normed, axis=0)), lax.optimization_barrier(jnp.sum(grad_first, axis=0)), lax.optimization_barrier(jnp.sum(grad_second * normed, axis=0)), lax.optimization_barrier(jnp.sum(grad_second, axis=0)), lax.optimization_barrier(jnp.sum(cot_rows, axis=0)), grad_qkv, lax.optimization_barrier(jnp.sum(grad_mixed, axis=0)), grad_dense, grad_up, lax.optimization_barrier(jnp.sum(grad_pre, axis=0)), grad_down)
        totals = jax.tree.map(lambda left, right: left + right, totals, terms)
        return (totals, (result, input_grad))
    start = (jnp.zeros((D,), jnp.float32), jnp.zeros((D,), jnp.float32), jnp.zeros((D,), jnp.float32), jnp.zeros((D,), jnp.float32), jnp.zeros((D,), jnp.float32), jnp.zeros((D, 3 * D), jnp.float32), jnp.zeros((3 * D,), jnp.float32), jnp.zeros((D, D), jnp.float32), jnp.zeros((D, FF), jnp.float32), jnp.zeros((FF,), jnp.float32), jnp.zeros((FF, D), jnp.float32))
    inputs = (hidden_in.reshape(-1, LEN, D), cotangent.reshape(-1, LEN, D), segment_ids)
    totals, outputs = lax.scan(one_sequence, start, inputs)
    hidden_out = outputs[0].reshape(-1, D)
    hidden_grad = outputs[1].reshape(-1, D)
    gain_one, shift_one, gain_two, shift_two, out_shift, grad_qkv, grad_qkv_bias, grad_dense, grad_up, grad_up_bias, grad_down = totals
    return (hidden_out, hidden_grad, gain_one, shift_one, gain_two, shift_two, grad_qkv, grad_qkv_bias.reshape(HEADS, 3 * HD), grad_dense, out_shift, grad_up, grad_up_bias.reshape(FF // BIAS_ROW, BIAS_ROW), grad_down, out_shift)
```

```python
import functools
import math

import jax
import jax.numpy as jnp
from jax import lax
from jax.experimental import pallas as pl
from jax.experimental.pallas import tpu as pltpu
from jax.sharding import PartitionSpec as P

HD = 64
ROT = 16
BIAS_ROW = 256
MAX_DOC = 256
QB = 128
norm_eps = 1e-05

BF = jnp.bfloat16
F32 = jnp.float32


def dot(a, b):
    return lax.dot_general(a, b, (((1,), (0,)), ((), ())), preferred_element_type=F32)


def dot_t(a, b):
    return lax.dot_general(a, b, (((1,), (1,)), ((), ())), preferred_element_type=F32)


def t_dot(a, b):
    return lax.dot_general(a, b, (((0,), (0,)), ((), ())), preferred_element_type=F32)


def vmem():
    return pltpu.CompilerParams(vmem_limit_bytes=60 * 1024 * 1024, dimension_semantics=("arbitrary",))


def whole(shape):
    zeros = (0,) * len(shape)
    return pl.BlockSpec(tuple(shape), lambda i, *_: zeros)


def swap(array, axis, size, bits):
    return lax.ppermute(array, axis, [(i, i ^ bits) for i in range(size)])


def hyper_sum(array, axis, size):
    step = 1
    while step < size:
        array = array + swap(array, axis, size, step)
        step *= 2
    return array


def hyper_gather(array, axis, size):
    place = lax.axis_index(axis)
    step = 1
    while step < size:
        other = swap(array, axis, size, step)
        high = (place // step) % 2 == 1
        array = jnp.concatenate(
            [jnp.where(high, other, array), jnp.where(high, array, other)], axis=0
        )
        step *= 2
    return array


def rotate(wide, cosine, sine_low, sine_high, sign):
    width = wide.shape[-1]
    half = ROT // 2
    down = pltpu.roll(wide, width - half, 1)
    up = pltpu.roll(wide, half, 1)
    return wide * cosine + sign * (down * sine_low + up * sine_high)


def assemble_body(place_ref, *refs):
    out = refs[-1]
    at = 0
    for ref in refs[:-1]:
        count, rows, _ = ref.shape
        for j in range(count):
            k = EXCHANGE[at]
            start = pl.multiple_of((place_ref[0] ^ k) * rows, 16)
            out[pl.ds(start, rows), :] = ref[j]
            at += 1


EXCHANGE = (0, 2, 4, 6, 1, 3, 5, 7)


def assemble(place, blocks):
    rows, cols = blocks[0].shape[1:]
    total = sum(b.shape[0] for b in blocks)
    return pl.pallas_call(
        assemble_body,
        grid_spec=pltpu.PrefetchScalarGridSpec(
            num_scalar_prefetch=1,
            grid=(1,),
            in_specs=[whole(b.shape) for b in blocks],
            out_specs=whole((total * rows, cols)),
        ),
        out_shape=jax.ShapeDtypeStruct((total * rows, cols), blocks[0].dtype),
        compiler_params=vmem(),
        name="assemble",
    )(place, *blocks)


def forward_in_body(
    z_ref, hid, gains, wa, wb, qb, ub, cosine, sine_low, sine_high,
    xhat_o, first_o, second_o, mixed_o, active_o, slope_o, scratch,
):
    qcols = qb.shape[1]
    x = hid[...].astype(F32)
    centre = jnp.mean(x, axis=-1, keepdims=True)
    cent = x - centre
    spread = jnp.mean(cent * cent, axis=-1, keepdims=True)
    xhat = cent * lax.rsqrt(spread + norm_eps)
    xhat_o[...] = xhat
    first = (xhat * gains[0:1, :] + gains[1:2, :]).astype(BF)
    second = (xhat * gains[2:3, :] + gains[3:4, :]).astype(BF)
    first_o[...] = first
    second_o[...] = second
    scratch[...] = jnp.zeros_like(scratch)
    scratch[:, :qcols] = dot(first, wa[:, :qcols]) + qb[...]
    turned = rotate(scratch[...], cosine[...], sine_low[...], sine_high[...], 1.0)
    mixed_o[...] = turned.astype(BF)
    fcols = ub.shape[1]
    pre = dot(second, wb[:, :fcols]) + ub[...]
    cumulative = 0.5 * (1.0 + lax.erf(pre * (1.0 / math.sqrt(2.0))))
    density = jnp.exp(-0.5 * pre * pre) * (1.0 / math.sqrt(2.0 * math.pi))
    active_o[...] = (pre * cumulative).astype(BF)
    slope_o[...] = cumulative + pre * density


def windows(length):
    reach = -(-(MAX_DOC - 1) // QB)
    return [(max(0, i - reach) * QB, (i + 1) * QB) for i in range(length // QB)]


def attend_fwd_body(mix, segc, segr, att_o, p_o, *, heads):
    length = mix.shape[0]
    for i, (lo, hi) in enumerate(windows(length)):
        width = hi - lo
        rows = lax.broadcasted_iota(jnp.int32, (QB, width), 0) + i * QB
        cols = lax.broadcasted_iota(jnp.int32, (QB, width), 1) + lo
        mask = (segc[i * QB : (i + 1) * QB, :] == segr[0, :, lo:hi]) & (rows >= cols)
        for h in range(heads):
            base = h * 3 * HD
            q = mix[i * QB : (i + 1) * QB, base : base + HD]
            k = mix[lo:hi, base + HD : base + 2 * HD]
            v = mix[lo:hi, base + 2 * HD : base + 3 * HD]
            s = jnp.where(mask, dot_t(q, k) * (HD**-0.5), -1e30)
            p = jnp.exp(s - jnp.max(s, axis=-1, keepdims=True))
            w = (p * (1.0 / jnp.sum(p, axis=-1, keepdims=True))).astype(BF)
            att_o[i * QB : (i + 1) * QB, h * HD : (h + 1) * HD] = dot(w, v).astype(BF)
            p_o[0, h, i, :, :width] = w


def forward_out_body(z_ref, att, act, wa, wb, out_o, *, qcols, fcols):
    out_o[0] = (dot_t(att[...], wa[:, qcols:]) + dot_t(act[...], wb[:, fcols:])).astype(BF)


def mlp_bwd_body(
    meta, cot, act, slope, second, xhat, gains, wb,
    n_o, gkeep_o, gsend_o, ub_o, stat_o, gup, gdown, *, fcols, blocks, split,
):
    step = pl.program_id(0)

    @pl.when(step == 0)
    def _():
        gup[...] = jnp.zeros_like(gup)
        gdown[...] = jnp.zeros_like(gdown)
        ub_o[...] = jnp.zeros_like(ub_o)
        stat_o[...] = jnp.zeros_like(stat_o)

    c = cot[0]
    gdown[...] += t_dot(c, act[...])
    gp = dot(c, wb[:, fcols:]) * slope[...]
    ub_o[0:1, :] += jnp.sum(gp, axis=0, keepdims=True)
    gph = gp.astype(BF)
    gup[...] += t_dot(second[...], gph)
    part = dot_t(gph, wb[:, :fcols])
    stat_o[0:1, :] += jnp.sum(part * xhat[...], axis=0, keepdims=True)
    stat_o[1:2, :] += jnp.sum(part, axis=0, keepdims=True)
    n_o[...] = part * gains[2:3, :]

    @pl.when(step == pl.num_programs(0) - 1)
    def _():
        emit(meta, (gup, gdown), gkeep_o, gsend_o, blocks, split)


def emit(meta, parts, keep_o, send_o, blocks, split):
    rows = keep_o.shape[1]
    for k in range(blocks):
        if split:
            start = pl.multiple_of((meta[1] ^ k) * rows, 16)
            target = send_o if k % 2 else keep_o
            slot = k // 2
        else:
            start, target, slot = k * rows, keep_o, k
        at = 0
        for part in parts:
            wide = part.shape[1]
            target[slot, :, at : at + wide] = part[pl.ds(start, rows), :].astype(target.dtype)
            at += wide


def attend_bwd_body(
    mix, p_in, cot, att, wa, cosine, sine_low, sine_high, gm_o, qb_o, gdense_o, dmix, *, heads, qcols,
):
    @pl.when(pl.program_id(0) == 0)
    def _():
        qb_o[...] = jnp.zeros_like(qb_o)
        gdense_o[...] = jnp.zeros_like(gdense_o)

    length = mix.shape[0]
    c = cot[...]
    gdense_o[...] += t_dot(c, att[...])
    ga = dot(c, wa[:, qcols:]).astype(BF)
    dmix[...] = jnp.zeros_like(dmix)
    for h in range(heads):
        base = h * 3 * HD
        for i, (lo, hi) in enumerate(windows(length)):
            width = hi - lo
            q = mix[i * QB : (i + 1) * QB, base : base + HD]
            k = mix[lo:hi, base + HD : base + 2 * HD]
            v = mix[lo:hi, base + 2 * HD : base + 3 * HD]
            g = ga[i * QB : (i + 1) * QB, h * HD : (h + 1) * HD]
            w = p_in[0, h, i, :, :width]
            wide = w.astype(F32)
            gw = dot_t(g, v)
            inner = jnp.sum(wide * gw, axis=-1, keepdims=True)
            ds = (wide * (gw - inner) * (HD**-0.5)).astype(BF)
            dmix[i * QB : (i + 1) * QB, base : base + HD] = dot(ds, k)
            dmix[lo:hi, base + HD : base + 2 * HD] += t_dot(ds, q)
            dmix[lo:hi, base + 2 * HD : base + 3 * HD] += t_dot(w, g)
    turned = rotate(dmix[...], cosine[...], sine_low[...], sine_high[...], -1.0)
    qb_o[0:1, :] += jnp.sum(turned, axis=0, keepdims=True)
    gm_o[...] = turned.astype(BF)


def qkv_bwd_body(
    meta, gm, first, xhat, gains, wa, n_in, gdense,
    n_o, gkeep_o, gsend_o, stat_o, gqkv, *, qcols, blocks, split,
):
    step = pl.program_id(0)

    @pl.when(step == 0)
    def _():
        gqkv[...] = jnp.zeros_like(gqkv)
        stat_o[...] = jnp.zeros_like(stat_o)

    g = gm[:, :qcols]
    gqkv[...] += t_dot(first[...], g)
    part = dot_t(g, wa[:, :qcols])
    stat_o[0:1, :] += jnp.sum(part * xhat[...], axis=0, keepdims=True)
    stat_o[1:2, :] += jnp.sum(part, axis=0, keepdims=True)
    n_o[0] = (part * gains[0:1, :] + n_in[...]).astype(BF)

    @pl.when(step == pl.num_programs(0) - 1)
    def _():
        emit(meta, (gqkv, gdense), gkeep_o, gsend_o, blocks, split)


def gather_weights(shard, place, dp):
    if dp != len(EXCHANGE) or shard.shape[0] % 16:
        return lax.all_gather(shard, "dp", axis=0, tiled=True)
    near = [shard] + [swap(shard, "dp", dp, k) for k in (2, 4, 6)]
    far = [swap(a, "dp", dp, 1) for a in near]
    return assemble(place, [a[None] for a in near + far])


def reduce_weights(keep, send, dp):
    if send is None:
        total = lax.psum_scatter(keep.astype(F32), "dp", scatter_dimension=0, tiled=True)
        return total[0]
    got = swap(send, "dp", dp, 1)
    near = keep.astype(F32) + got.astype(F32)
    total = near[0]
    for j in range(1, near.shape[0]):
        total = total + swap(near[j].astype(BF), "dp", dp, 2 * j).astype(F32)
    return total


def gather_tokens(own, tensor):
    if tensor != 4:
        every = lax.all_gather(own, "tensor", axis=0)
        order = lax.axis_index("tensor") ^ jnp.arange(tensor)
        return jnp.take(every, order, axis=0)
    two = swap(own, "tensor", tensor, 2)
    one = swap(own, "tensor", tensor, 1)
    three = swap(two, "tensor", tensor, 1)
    return jnp.stack([own, one, two, three])


def scatter_tokens(parts, tensor):
    if tensor != 4:
        total = parts[0].astype(F32)
        for k in range(1, tensor):
            total = total + swap(parts[k], "tensor", tensor, k).astype(F32)
        return total
    relay = swap(parts[3], "tensor", tensor, 1)
    one = swap(parts[1], "tensor", tensor, 1)
    pair = (parts[2].astype(F32) + relay.astype(F32)).astype(BF)
    two = swap(pair, "tensor", tensor, 2)
    return parts[0].astype(F32) + one.astype(F32) + two.astype(F32)


def rotary_tables(length, heads, width):
    place = jnp.arange(length).astype(F32)[:, None]
    lane = jnp.arange(width)
    entry = lane % HD
    half = ROT // 2
    turns = (entry < ROT) & ((lane // HD) % 3 < 2) & (lane < heads * 3 * HD)
    index = (entry % half).astype(F32) * 2.0
    frequency = 1.0 / 10000.0 ** (index / ROT)
    angle = place * frequency[None, :]
    cosine = jnp.where(turns[None, :], jnp.cos(angle), 1.0)
    sine = jnp.where(turns[None, :], jnp.sin(angle), 0.0)
    low = (entry < half)[None, :]
    return cosine, jnp.where(low, -sine, 0.0), jnp.where(low, 0.0, sine)


def on_device(
    hidden_in, segment_ids, cotangent, norm1_gain, norm1_bias, norm2_gain, norm2_bias,
    qkv_weight, qkv_bias, dense_weight, dense_bias, up_weight, up_bias, down_weight, down_bias,
    *, dp, tensor,
):
    d_at = lax.axis_index("dp")
    z_at = lax.axis_index("tensor")
    meta = jnp.stack([z_at, d_at]).astype(jnp.int32)
    place = d_at.astype(jnp.int32)[None]
    tokens, width = hidden_in.shape
    total = tokens * tensor
    seqs, length = segment_ids.shape
    qcols = qkv_weight.shape[1]
    heads = qcols // (3 * HD)
    acols = heads * HD
    fcols = up_weight.shape[1]
    qwide = -(-qcols // 128) * 128
    rows = width // dp
    split = dp == len(EXCHANGE) and rows % 16 == 0
    blk = min(256, tokens)
    per = tokens // blk
    steps = total // blk

    hid_rel = gather_tokens(hidden_in, tensor)
    pack_a = jnp.concatenate([qkv_weight, dense_weight.T], axis=1)
    pack_b = jnp.concatenate([up_weight, down_weight.T], axis=1)
    wa = gather_weights(pack_a, place, dp)
    wb = gather_weights(pack_b, place, dp)

    vecs = jnp.stack([norm1_gain, norm1_bias, norm2_gain, norm2_bias, dense_bias, down_bias])
    nvec, part = vecs.shape
    small = jnp.concatenate(
        [vecs.reshape(-1), qkv_bias.astype(F32).reshape(-1), up_bias.astype(F32).reshape(-1)]
    )[None]
    small = hyper_gather(small, "dp", dp)
    nv = nvec * part
    nq = qkv_bias.size
    vec_all = hyper_gather(small[None, :, :nv], "tensor", tensor)
    gains = (
        vec_all.reshape(tensor, dp, nvec, part).transpose(2, 1, 0, 3).reshape(nvec, width)
    )
    qb = small[:, nv : nv + nq].reshape(dp, heads, -1).transpose(1, 0, 2).reshape(1, qcols)
    ub = (
        small[:, nv + nq :].reshape(dp, up_bias.shape[0], -1).transpose(1, 0, 2).reshape(1, fcols)
    )
    cosine, sine_low, sine_high = rotary_tables(length, heads, qwide)

    half = cotangent.astype(BF)
    half, hid_rel = lax.optimization_barrier((half, hid_rel))
    cot_rel = gather_tokens(half, tensor)

    def rel(i, meta_ref):
        return ((i // per) ^ meta_ref[0]) * per + i % per

    def tok(cols):
        return pl.BlockSpec((blk, cols), lambda i, m: (i, 0))

    def tok_rel(cols):
        return pl.BlockSpec((1, blk, cols), lambda i, m: (rel(i, m), 0, 0))

    def tab():
        n = length // blk
        return pl.BlockSpec((blk, qwide), lambda i, m: (i % n, 0))

    def sds(shape, dtype):
        return jax.ShapeDtypeStruct(shape, dtype)

    xhat, first, second, mixed, active, slope = pl.pallas_call(
        forward_in_body,
        grid_spec=pltpu.PrefetchScalarGridSpec(
            num_scalar_prefetch=1,
            grid=(steps,),
            in_specs=[
                pl.BlockSpec((None, blk, width), lambda i, m: (rel(i, m), 0, 0)),
                whole(gains.shape), whole(wa.shape), whole(wb.shape), whole(qb.shape),
                whole(ub.shape), tab(), tab(), tab(),
            ],
            out_specs=[tok(width), tok(width), tok(width), tok(qwide), tok(fcols), tok(fcols)],
            scratch_shapes=[pltpu.VMEM((blk, qwide), F32)],
        ),
        out_shape=[
            sds((total, width), F32), sds((total, width), BF), sds((total, width), BF),
            sds((total, qwide), BF), sds((total, fcols), BF), sds((total, fcols), F32),
        ],
        compiler_params=vmem(),
        name="forward_in",
    )(meta, hid_rel.reshape(steps, blk, width), gains, wa, wb, qb, ub, cosine, sine_low, sine_high)

    nwin = length // QB
    wwin = max(hi - lo for lo, hi in windows(length))
    segc = segment_ids.reshape(total, 1)
    segr = segment_ids.reshape(seqs, 1, length)

    def seq(cols):
        return pl.BlockSpec((length, cols), lambda r: (r, 0))

    p_spec = pl.BlockSpec((1, heads, nwin, QB, wwin), lambda r: (r, 0, 0, 0, 0))
    attended, weights = pl.pallas_call(
        functools.partial(attend_fwd_body, heads=heads),
        grid=(seqs,),
        in_specs=[seq(qwide), seq(1), pl.BlockSpec((1, 1, length), lambda r: (r, 0, 0))],
        out_specs=[seq(acols), p_spec],
        out_shape=[sds((total, acols), BF), sds((seqs, heads, nwin, QB, wwin), BF)],
        compiler_params=vmem(),
        name="attend_fwd",
    )(mixed, segc, segr)

    def tok_can(cols):
        return pl.BlockSpec((blk, cols), lambda i, m: (rel(i, m), 0))

    def out_rel(cols):
        return pl.BlockSpec((1, blk, cols), lambda i, m: (i, 0, 0))

    out_parts = pl.pallas_call(
        functools.partial(forward_out_body, qcols=qcols, fcols=fcols),
        grid_spec=pltpu.PrefetchScalarGridSpec(
            num_scalar_prefetch=1,
            grid=(steps,),
            in_specs=[tok_can(acols), tok_can(fcols), whole(wa.shape), whole(wb.shape)],
            out_specs=out_rel(width),
        ),
        out_shape=sds((steps, blk, width), BF),
        compiler_params=vmem(),
        name="forward_out",
    )(meta, attended, active, wa, wb)
    branch = scatter_tokens(out_parts.reshape(tensor, tokens, width), tensor)
    wide_rows = hidden_in.astype(F32)
    hidden_out = wide_rows + branch + gains[4] + gains[5]

    cot_steps = cot_rel.reshape(steps, blk, width)
    nblk = dp
    if split:
        half_blocks = (nblk // 2, rows)
    else:
        half_blocks = (nblk, rows)

    def grad_shapes(cols):
        kept = sds(half_blocks + (cols,), F32)
        sent = sds(half_blocks + (cols,), BF) if split else sds((1, 16, 128), BF)
        return kept, sent

    bk, bs = grad_shapes(2 * fcols)
    n_two, b_keep, b_send, ub_sum, stat_two = pl.pallas_call(
        functools.partial(mlp_bwd_body, fcols=fcols, blocks=nblk, split=split),
        grid_spec=pltpu.PrefetchScalarGridSpec(
            num_scalar_prefetch=1,
            grid=(steps,),
            in_specs=[
                tok_rel(width), tok(fcols), tok(fcols), tok(width), tok(width),
                whole(gains.shape), whole(wb.shape),
            ],
            out_specs=[tok(width), whole(bk.shape), whole(bs.shape), whole((8, fcols)), whole((8, width))],
            scratch_shapes=[pltpu.VMEM((width, fcols), F32), pltpu.VMEM((width, fcols), F32)],
        ),
        out_shape=[sds((total, width), F32), bk, bs, sds((8, fcols), F32), sds((8, width), F32)],
        compiler_params=vmem(),
        name="mlp_bwd",
    )(meta, cot_steps, active, slope, second, xhat, gains, wb)

    order = jnp.arange(tensor) ^ z_at
    cot_can = jnp.take(cot_rel, order, axis=0).reshape(total, width)
    gm, qb_sum, gdense = pl.pallas_call(
        functools.partial(attend_bwd_body, heads=heads, qcols=qcols),
        grid=(seqs,),
        in_specs=[
            seq(qwide), p_spec, seq(width), seq(acols), whole(wa.shape),
            whole(cosine.shape), whole(cosine.shape), whole(cosine.shape),
        ],
        out_specs=[seq(qwide), whole((8, qwide)), whole((width, acols))],
        out_shape=[sds((total, qwide), BF), sds((8, qwide), F32), sds((width, acols), F32)],
        scratch_shapes=[pltpu.VMEM((length, qwide), F32)],
        compiler_params=vmem(),
        name="attend_bwd",
    )(mixed, weights, cot_can, attended, wa, cosine, sine_low, sine_high)

    ak, as_ = grad_shapes(qcols + acols)
    n_parts, a_keep, a_send, stat_one = pl.pallas_call(
        functools.partial(qkv_bwd_body, qcols=qcols, blocks=nblk, split=split),
        grid_spec=pltpu.PrefetchScalarGridSpec(
            num_scalar_prefetch=1,
            grid=(steps,),
            in_specs=[
                tok_can(qwide), tok_can(width), tok_can(width), whole(gains.shape), whole(wa.shape),
                tok_can(width), whole(gdense.shape),
            ],
            out_specs=[out_rel(width), whole(ak.shape), whole(as_.shape), whole((8, width))],
            scratch_shapes=[pltpu.VMEM((width, qcols), F32)],
        ),
        out_shape=[sds((steps, blk, width), BF), ak, as_, sds((8, width), F32)],
        compiler_params=vmem(),
        name="qkv_bwd",
    )(meta, gm, first, xhat, gains, wa, n_two, gdense)

    grad_normed = scatter_tokens(n_parts.reshape(tensor, tokens, width), tensor)
    b_grad = reduce_weights(b_keep, b_send if split else None, dp)
    a_grad = reduce_weights(a_keep, a_send if split else None, dp)

    centre = jnp.mean(wide_rows, axis=-1, keepdims=True)
    cent = wide_rows - centre
    inverse = lax.rsqrt(jnp.mean(cent * cent, axis=-1, keepdims=True) + norm_eps)
    normed = cent * inverse
    hidden_grad = cotangent + inverse * (
        grad_normed
        - jnp.mean(grad_normed, axis=-1, keepdims=True)
        - normed * jnp.mean(grad_normed * normed, axis=-1, keepdims=True)
    )

    stats = jnp.concatenate(
        [stat_one[:2], stat_two[:2], jnp.sum(cotangent, axis=0)[None]], axis=0
    )
    flat = jnp.concatenate([stats.reshape(-1), qb_sum[0, :qcols], ub_sum[0]])
    pad = -flat.size % 1024
    flat = jnp.pad(flat, (0, pad)).reshape(-1, 128)
    flat = hyper_sum(flat, "dp", dp).reshape(-1)
    nstat = stats.size
    qb_all = flat[nstat : nstat + qcols].reshape(heads, dp, -1)
    ub_all = flat[nstat + qcols : nstat + qcols + fcols].reshape(up_bias.shape[0], dp, -1)
    qb_grad = lax.dynamic_index_in_dim(qb_all, d_at, 1, keepdims=False)
    ub_grad = lax.dynamic_index_in_dim(ub_all, d_at, 1, keepdims=False)
    mine = lax.dynamic_index_in_dim(flat[:nstat].reshape(5, dp, -1), d_at, 1, keepdims=False)
    mine = hyper_sum(mine, "tensor", tensor)
    mine = lax.dynamic_index_in_dim(mine.reshape(5, tensor, part), z_at, 1, keepdims=False)

    return (
        hidden_out,
        hidden_grad,
        mine[0],
        mine[1],
        mine[2],
        mine[3],
        a_grad[:, :qcols],
        qb_grad,
        a_grad[:, qcols:].T,
        mine[4],
        b_grad[:, :fcols],
        ub_grad,
        b_grad[:, fcols:].T,
        mine[4],
    )


def solution(mesh):
    both = P(("dp", "tensor"))
    wide = P(("dp", "tensor"), None)
    return jax.shard_map(
        functools.partial(on_device, dp=mesh.shape["dp"], tensor=mesh.shape["tensor"]),
        mesh=mesh,
        in_specs=(
            wide, P("dp", None), wide, both, both, both, both, P("dp", "tensor"),
            P("tensor", "dp"), P("tensor", "dp"), both, P("dp", "tensor"), P("tensor", "dp"),
            P("tensor", "dp"), both,
        ),
        out_specs=(
            wide, wide, both, both, both, both, P("dp", "tensor"), P("tensor", "dp"),
            P("tensor", "dp"), both, P("dp", "tensor"), P("tensor", "dp"), P("tensor", "dp"), both,
        ),
        check_vma=False,
    )
```

```python
import functools
import math

import jax
import jax.numpy as jnp
from jax import lax
from jax.experimental import pallas as pl
from jax.experimental.pallas import tpu as pltpu
from jax.sharding import PartitionSpec as P


HD = 64
ROT = 16
MAX_DOC = 256
QB = 128
norm_eps = 1e-05

BF = jnp.bfloat16
F32 = jnp.float32


def dot(a, b):
    return lax.dot_general(a, b, (((1,), (0,)), ((), ())), preferred_element_type=F32)


def dot_t(a, b):
    return lax.dot_general(a, b, (((1,), (1,)), ((), ())), preferred_element_type=F32)


def t_dot(a, b):
    return lax.dot_general(a, b, (((0,), (0,)), ((), ())), preferred_element_type=F32)


def vmem():
    return pltpu.CompilerParams(vmem_limit_bytes=60 * 1024 * 1024)


def whole(shape):
    zeros = (0,) * len(shape)
    return pl.BlockSpec(tuple(shape), lambda i, *_: zeros)


def swap(array, axis, size, bits):
    return lax.ppermute(array, axis, [(i, i ^ bits) for i in range(size)])


def hyper_gather(array, axis, size):
    place = lax.axis_index(axis)
    step = 1
    while step < size:
        other = swap(array, axis, size, step)
        high = (place // step) % 2 == 1
        array = jnp.concatenate(
            [jnp.where(high, other, array), jnp.where(high, array, other)], axis=0
        )
        step *= 2
    return array


def rotate(wide, tables, sign):
    width = wide.shape[-1]
    half = ROT // 2
    lane = lax.broadcasted_iota(jnp.int32, (1, width), 1)
    turns = ((lane // HD) % 3 < 2).astype(F32)
    reps = width // tables.shape[-1]
    cosine, low, high = (jnp.concatenate([tables[j]] * reps, axis=1) * turns for j in range(3))
    down = pltpu.roll(wide, width - half, 1)
    up = pltpu.roll(wide, half, 1)
    return wide + wide * cosine + sign * (down * low + up * high)


def assemble_body(place_ref, *refs):
    out = refs[-1]
    at = 0
    for ref in refs[:-1]:
        count, rows, _ = ref.shape
        for j in range(count):
            k = EXCHANGE[at]
            start = pl.multiple_of((place_ref[0] ^ k) * rows, 16)
            out[pl.ds(start, rows), :] = ref[j]
            at += 1


EXCHANGE = (0, 2, 4, 6, 1, 3, 5, 7)


def assemble(place, blocks):
    rows, cols = blocks[0].shape[1:]
    total = sum(b.shape[0] for b in blocks)
    return pl.pallas_call(
        assemble_body,
        grid_spec=pltpu.PrefetchScalarGridSpec(
            num_scalar_prefetch=1,
            grid=(1,),
            in_specs=[whole(b.shape) for b in blocks],
            out_specs=whole((total * rows, cols)),
        ),
        out_shape=jax.ShapeDtypeStruct((total * rows, cols), blocks[0].dtype),
        compiler_params=vmem(),
        name="assemble",
    )(place, *blocks)


def windows(length):
    reach = -(-(MAX_DOC - 1) // QB)
    return [(max(0, i - reach) * QB, (i + 1) * QB) for i in range(length // QB)]


def spot(meta, a, tokens):
    return pl.ds(pl.multiple_of(((meta[0] % 2) ^ a) * tokens, tokens), tokens)


def attn_fwd_body(
    meta, hid_a, hid_b, gains, wa, qb, tables, segc, segr,
    xhat_o, first_o, second_o, mixed_o, att_o, p_o, scratch,
):
    qcols = qb.shape[1]
    tokens = hid_a.shape[0]
    for a, hid in enumerate((hid_a, hid_b)):
        at = spot(meta, a, tokens)
        x = hid[...].astype(F32)
        cent = x - jnp.mean(x, axis=-1, keepdims=True)
        spread = jnp.mean(cent * cent, axis=-1, keepdims=True)
        xhat = cent * lax.rsqrt(spread + norm_eps)
        xhat_o[at, :] = xhat.astype(BF)
        first_o[at, :] = (xhat * gains[0:1, :] + gains[1:2, :]).astype(BF)
        second_o[at, :] = (xhat * gains[2:3, :] + gains[3:4, :]).astype(BF)
    seqs, _, length = segr.shape
    heads = qcols // (3 * HD)
    scratch[...] = jnp.zeros_like(scratch)
    for r in range(seqs):
        row = slice(r * length, (r + 1) * length)
        scratch[:, :qcols] = dot(first_o[row, :], wa[:, :qcols]) + qb[...]
        mixed_o[row, :] = rotate(scratch[...], tables, 1.0).astype(BF)
    for r in range(seqs):
        start = r * length
        for i, (lo, hi) in enumerate(windows(length)):
            width = hi - lo
            qs = slice(start + i * QB, start + (i + 1) * QB)
            ks = slice(start + lo, start + hi)
            rows = lax.broadcasted_iota(jnp.int32, (QB, width), 0) + i * QB
            cols = lax.broadcasted_iota(jnp.int32, (QB, width), 1) + lo
            mask = (segc[qs, :] == segr[r, :, lo:hi]) & (rows >= cols)
            for h in range(heads):
                base = h * 3 * HD
                q = mixed_o[qs, base : base + HD]
                k = mixed_o[ks, base + HD : base + 2 * HD]
                v = mixed_o[ks, base + 2 * HD : base + 3 * HD]
                s = jnp.where(mask, dot_t(q, k) * (HD**-0.5), -1e30)
                p = jnp.exp(s - jnp.max(s, axis=-1, keepdims=True))
                w = (p * (1.0 / jnp.sum(p, axis=-1, keepdims=True))).astype(BF)
                att_o[qs, h * HD : (h + 1) * HD] = dot(w, v).astype(BF)
                p_o[r, h, i, :, :width] = w


def mlp_fwd_body(meta, second, att, wa, wb, ub, active_o, slope_o, out_o, *, qcols):
    fcols = ub.shape[1]
    tokens = out_o.shape[1]
    for a in range(2):
        at = spot(meta, a, tokens)
        pre = dot(second[at, :], wb[:, :fcols]) + ub[...]
        cumulative = 0.5 * (1.0 + lax.erf(pre * (1.0 / math.sqrt(2.0))))
        density = jnp.exp(-0.5 * pre * pre) * (1.0 / math.sqrt(2.0 * math.pi))
        act = (pre * cumulative).astype(BF)
        active_o[at, :] = act
        slope_o[at, :] = (cumulative + pre * density).astype(BF)
        out_o[a] = (dot_t(att[at, :], wa[:, qcols:]) + dot_t(act, wb[:, fcols:])).astype(BF)


def mlp_bwd_body(
    meta, cots, halves, gains, wb, n_o, gkeep_o, gsend_o, ub_o, stat_o, gup, gdown,
    *, fcols, blocks, split,
):
    tokens = cots[0].shape[0]
    first_pass = True
    for half in range(2):
        act, slope, second, xhat = halves[half]
        for a in range(2):
            at = spot(meta, a, tokens)
            c = cots[2 * half + a][...]
            down = t_dot(c, act[at, :])
            gp = dot(c, wb[:, fcols:]) * slope[at, :].astype(F32)
            gph = gp.astype(BF)
            up = t_dot(second[at, :], gph)
            part = dot_t(gph, wb[:, :fcols])
            sums = (
                jnp.sum(gp, axis=0, keepdims=True),
                jnp.sum(part * xhat[at, :].astype(F32), axis=0, keepdims=True),
                jnp.sum(part, axis=0, keepdims=True),
            )
            n_o[half, at, :] = (part * gains[2:3, :]).astype(BF)
            if first_pass:
                gdown[...] = down
                gup[...] = up
                ub_o[0:1, :] = sums[0]
                stat_o[0:1, :] = sums[1]
                stat_o[1:2, :] = sums[2]
            else:
                gdown[...] += down
                gup[...] += up
                ub_o[0:1, :] += sums[0]
                stat_o[0:1, :] += sums[1]
                stat_o[1:2, :] += sums[2]
            first_pass = False
    emit(meta, (gup, gdown), gkeep_o, gsend_o, blocks, split)


def emit(meta, parts, keep_o, send_o, blocks, split):
    rows = keep_o.shape[1]
    for k in range(blocks):
        if split:
            start = pl.multiple_of((meta[1] ^ k) * rows, 16)
            target = send_o if k % 2 else keep_o
            slot = k // 2
        else:
            start, target, slot = k * rows, keep_o, k
        at = 0
        for part in parts:
            wide = part.shape[1]
            target[slot, :, at : at + wide] = part[pl.ds(start, rows), :].astype(target.dtype)
            at += wide


def attn_bwd_body(
    meta, cot_a, cot_b, mix, p_in, att, first, xhat, n_in, gains, wa, tables,
    n_o, stat_o, qb_o, gqkv, gdense, dmix, cot, *, heads, qcols, seqs, last,
):
    tokens = cot_a.shape[0]
    for a, ref in enumerate((cot_a, cot_b)):
        cot[spot(meta, a, tokens), :] = ref[...]
    c = cot[...]
    length = c.shape[0] // seqs
    down = t_dot(c, att[...])
    gdense[...] = down if last is None else last[1][...] + down
    ga = dot(c, wa[:, qcols:]).astype(BF)
    dmix[...] = jnp.zeros_like(dmix)
    for r in range(seqs):
        start = r * length
        for h in range(heads):
            base = h * 3 * HD
            for i, (lo, hi) in enumerate(windows(length)):
                width = hi - lo
                qs = slice(start + i * QB, start + (i + 1) * QB)
                ks = slice(start + lo, start + hi)
                q = mix[qs, base : base + HD]
                k = mix[ks, base + HD : base + 2 * HD]
                v = mix[ks, base + 2 * HD : base + 3 * HD]
                g = ga[qs, h * HD : (h + 1) * HD]
                w = p_in[r, h, i, :, :width]
                wide = w.astype(F32)
                gw = dot_t(g, v)
                inner = jnp.sum(wide * gw, axis=-1, keepdims=True)
                ds = (wide * (gw - inner) * (HD**-0.5)).astype(BF)
                dmix[qs, base : base + HD] = dot(ds, k)
                dmix[ks, base + HD : base + 2 * HD] += t_dot(ds, q)
                dmix[ks, base + 2 * HD : base + 3 * HD] += t_dot(w, g)
        row = slice(start, start + length)
        dmix[row, :] = rotate(dmix[row, :], tables, -1.0)
    turned = dmix[...]
    total = jnp.sum(turned, axis=0, keepdims=True)
    qb_o[0:1, :] = total if last is None else last[3][0:1, :] + total
    g = turned[:, :qcols].astype(BF)
    up = t_dot(first[...], g)
    gqkv[...] = up if last is None else last[0][...] + up
    part = dot_t(g, wa[:, :qcols])
    sums = (
        jnp.sum(part * xhat[...].astype(F32), axis=0, keepdims=True),
        jnp.sum(part, axis=0, keepdims=True),
    )
    for j in range(2):
        stat_o[j : j + 1, :] = sums[j] if last is None else last[2][j : j + 1, :] + sums[j]
    dmix_n = part * gains[0:1, :] + n_in[0].astype(F32)
    cot[...] = dmix_n.astype(BF)
    for a in range(2):
        n_o[a] = cot[spot(meta, a, tokens), :]


def pack_body(meta, gqkv, gdense, stat, extra, qb, keep_o, send_o, wide, cols, *, blocks, split, heads):
    rows = keep_o.shape[1]
    lanes = cols.shape[1]
    wide[...] = jnp.zeros_like(wide)
    wide[0:2, :] = stat[0:2, :]
    wide[2:8, :] = extra[2:8, :]
    cols[...] = wide[...].T
    per = 3 * HD // blocks
    tall = jnp.broadcast_to(qb[0:1, :], (lanes, qb.shape[1])).T
    lane = lax.broadcasted_iota(jnp.int32, (per, lanes), 1)
    for d in range(blocks):
        for h in range(heads):
            at = slice(d * rows + h * per, d * rows + (h + 1) * per)
            src = tall[h * 3 * HD + d * per : h * 3 * HD + (d + 1) * per, :]
            cols[at, :] = jnp.where(lane == 7, src, cols[at, :])
    emit(meta, (gqkv, gdense, cols), keep_o, send_o, blocks, split)


def gather_weights(shard, place, dp):
    if dp != len(EXCHANGE) or shard.shape[0] % 16:
        return lax.all_gather(shard, "dp", axis=0, tiled=True)
    got = {k: swap(shard, "dp", dp, k) for k in (6, 2, 4)}
    near = [shard] + [got[k] for k in (2, 4, 6)]
    far = [swap(a, "dp", dp, 1) for a in near]
    return assemble(place, [a[None] for a in near + far])


def reduce_weights(keep, send, dp):
    if send is None:
        total = lax.psum_scatter(keep, "dp", scatter_dimension=0, tiled=True)
        return total[0]
    got = swap(send, "dp", dp, 1)
    near = [keep[j].astype(F32) + got[j].astype(F32) for j in range(keep.shape[0])]
    total = near[0]
    for j in (3, 1, 2):
        total = total + swap(near[j].astype(BF), "dp", dp, 2 * j).astype(F32)
    return total


def rotary_tables(length):
    place = jnp.arange(length).astype(F32)[:, None]
    entry = jnp.arange(128) % HD
    half = ROT // 2
    turns = (entry < ROT)[None, :]
    frequency = 1.0 / 10000.0 ** ((entry % half).astype(F32) * 2.0 / ROT)
    angle = place * frequency[None, :]
    cosine = jnp.where(turns, jnp.cos(angle) - 1.0, 0.0)
    sine = jnp.where(turns, jnp.sin(angle), 0.0)
    low = (entry < half)[None, :]
    return jnp.stack([cosine, jnp.where(low, -sine, 0.0), jnp.where(low, 0.0, sine)])


def call(body, out_shape, scratch, *args):
    return pl.pallas_call(
        body,
        grid_spec=pltpu.PrefetchScalarGridSpec(
            num_scalar_prefetch=1,
            grid=(1,),
            in_specs=[whole(a.shape) for a in args[1:]],
            out_specs=[whole(o.shape) for o in out_shape],
            scratch_shapes=[pltpu.VMEM(shape, dtype) for shape, dtype in scratch],
        ),
        out_shape=out_shape,
        compiler_params=vmem(),
    )(*args)


def block(
    hidden_in, segment_ids, cotangent, norm1_gain, norm1_bias, norm2_gain, norm2_bias,
    qkv_weight, qkv_bias, dense_weight, dense_bias, up_weight, up_bias, down_weight, down_bias,
    *, dp, tensor,
):
    d_at = lax.axis_index("dp")
    z_at = lax.axis_index("tensor")
    meta = jnp.stack([z_at, d_at]).astype(jnp.int32)
    place = d_at.astype(jnp.int32)[None]
    tokens, width = hidden_in.shape
    seqs, length = segment_ids.shape
    hseqs = seqs // 2
    htok = tokens * tensor // 2
    qcols = qkv_weight.shape[1]
    heads = qcols // (3 * HD)
    acols = heads * HD
    fcols = up_weight.shape[1]
    qwide = -(-qcols // 128) * 128
    rows = width // dp
    split = dp == len(EXCHANGE) and rows % 16 == 0
    stat_lanes = 128

    def sds(shape, dtype=F32):
        return jax.ShapeDtypeStruct(shape, dtype)

    def zswap(a, bits):
        return swap(a, "tensor", tensor, bits)

    hid_two = zswap(hidden_in, 2)
    hid_one = zswap(hidden_in, 1)
    pack_a = jnp.concatenate([qkv_weight, dense_weight.T], axis=1)
    pack_b = jnp.concatenate([up_weight, down_weight.T], axis=1)
    wa = gather_weights(pack_a, place, dp)
    wb = gather_weights(pack_b, place, dp)
    hid_three = zswap(hid_two, 1)
    half_cot = cotangent.astype(BF)
    cot_two = zswap(half_cot, 2)
    cot_one = zswap(half_cot, 1)
    cot_three = zswap(cot_two, 1)

    vecs = jnp.stack([norm1_gain, norm1_bias, norm2_gain, norm2_bias, dense_bias, down_bias])
    nvec, part = vecs.shape
    small = jnp.concatenate(
        [vecs.reshape(-1), qkv_bias.astype(F32).reshape(-1), up_bias.astype(F32).reshape(-1)]
    )[None]
    small = hyper_gather(small, "dp", dp)
    nv = nvec * part
    nq = qkv_bias.size
    vec_all = hyper_gather(small[None, :, :nv], "tensor", tensor)
    gains = (
        vec_all.reshape(tensor, dp, nvec, part).transpose(2, 1, 0, 3).reshape(nvec, width)
    )
    qb = small[:, nv : nv + nq].reshape(dp, heads, -1).transpose(1, 0, 2).reshape(1, qcols)
    ub = (
        small[:, nv + nq :].reshape(dp, up_bias.shape[0], -1).transpose(1, 0, 2).reshape(1, fcols)
    )
    tables = rotary_tables(length)

    side = z_at // 2
    near_ids = lax.dynamic_slice_in_dim(segment_ids, side * hseqs, hseqs, 0)
    far_ids = lax.dynamic_slice_in_dim(segment_ids, (1 - side) * hseqs, hseqs, 0)
    nwin = length // QB
    wwin = max(hi - lo for lo, hi in windows(length))

    def forward(hid_a, hid_b, ids):
        fa = call(
            attn_fwd_body,
            [
                sds((htok, width), BF), sds((htok, width), BF), sds((htok, width), BF),
                sds((htok, qwide), BF), sds((htok, acols), BF), sds((hseqs, heads, nwin, QB, wwin), BF),
            ],
            [((htok, qwide), F32)],
            meta, hid_a, hid_b, gains, wa, qb, tables, ids.reshape(htok, 1),
            ids.reshape(hseqs, 1, length),
        )
        xhat, first, second, mixed, att, weights = fa
        active, slope, out = call(
            functools.partial(mlp_fwd_body, qcols=qcols),
            [sds((htok, fcols), BF), sds((htok, fcols), BF), sds((2, tokens, width), BF)],
            [], meta, second, att, wa, wb, ub,
        )
        return dict(
            xhat=xhat, first=first, second=second, mixed=mixed, att=att, weights=weights,
            active=active, slope=slope, out=out,
        )

    near = forward(hidden_in, hid_one, near_ids)
    far = forward(hid_two, hid_three, far_ids)

    def scatter(near_parts, far_parts):
        relay = zswap(far_parts[1], 1)
        pair = (far_parts[0].astype(F32) + relay.astype(F32)).astype(BF)
        two = zswap(pair, 2)
        one = zswap(near_parts[1], 1)
        return near_parts[0].astype(F32) + one.astype(F32) + two.astype(F32)

    branch = scatter(near["out"], far["out"])
    wide_rows = hidden_in.astype(F32)
    hidden_out = wide_rows + branch + gains[4] + gains[5]

    if split:
        half_blocks = (dp // 2, rows)
    else:
        half_blocks = (dp, rows)

    def grad_shapes(cols):
        return [sds(half_blocks + (cols,)), sds(half_blocks + (cols,) if split else (1, 16, 128), BF)]

    def mlp_bwd(*refs):
        ins, outs = refs[:15], refs[15:]
        cots = ins[1:5]
        halves = (ins[5:9], ins[9:13])
        mlp_bwd_body(
            ins[0], cots, halves, ins[13], ins[14], *outs, fcols=fcols, blocks=dp, split=split
        )

    keys = ("active", "slope", "second", "xhat")
    n_mlp, b_keep, b_send, ub_sum, stat_two = call(
        mlp_bwd,
        [sds((2, htok, width), BF), *grad_shapes(2 * fcols), sds((8, fcols)), sds((8, width))],
        [((width, fcols), F32), ((width, fcols), F32)],
        meta, half_cot, cot_one, cot_two, cot_three, *(near[k] for k in keys), *(far[k] for k in keys),
        gains, wb,
    )

    def attn_bwd(cot_a, cot_b, kept, n_half, before):
        fixed = 12

        def body(*refs):
            ins = refs[:fixed]
            last = None if before is None else (refs[fixed], refs[fixed + 1], refs[fixed + 2], refs[fixed + 3])
            outs = refs[fixed + (0 if before is None else 4) :]
            attn_bwd_body(*ins, *outs, heads=heads, qcols=qcols, seqs=hseqs, last=last)

        return call(
            body,
            [
                sds((2, tokens, width), BF), sds((8, width)), sds((8, qwide)),
                sds((width, qcols)), sds((width, acols)),
            ],
            [((htok, qwide), F32), ((htok, width), BF)],
            meta, cot_a, cot_b, kept["mixed"], kept["weights"], kept["att"], kept["first"], kept["xhat"],
            n_half, gains, wa, tables, *(() if before is None else before),
        )

    n_far, s_far, q_far, gqkv_far, gdense_far = attn_bwd(cot_two, cot_three, far, n_mlp[1:2], None)
    n_near, stat_one, qb_sum, gqkv, gdense = attn_bwd(
        half_cot, cot_one, near, n_mlp[0:1], (gqkv_far, gdense_far, s_far, q_far)
    )
    ub_rows = ub_sum[0].reshape(up_bias.shape[0], dp, -1).transpose(1, 0, 2).reshape(dp, -1)
    ub_rows = jnp.pad(ub_rows, ((0, 0), (0, rows - ub_rows.shape[1]))).reshape(1, width)
    zero = jnp.zeros((2, width), F32)
    extra = jnp.concatenate(
        [zero, stat_two[:2], jnp.sum(cotangent, axis=0)[None], ub_rows, zero], axis=0
    )
    a_keep, a_send = call(
        functools.partial(pack_body, blocks=dp, split=split, heads=heads),
        grad_shapes(qcols + acols + stat_lanes),
        [((stat_lanes, width), F32), ((width, stat_lanes), F32)],
        meta, gqkv, gdense, stat_one, extra, qb_sum,
    )

    b_grad = reduce_weights(b_keep, b_send if split else None, dp)
    grad_normed = scatter(n_near, n_far)
    a_grad = reduce_weights(a_keep, a_send if split else None, dp)

    centre = jnp.mean(wide_rows, axis=-1, keepdims=True)
    cent = wide_rows - centre
    inverse = lax.rsqrt(jnp.mean(cent * cent, axis=-1, keepdims=True) + norm_eps)
    normed = cent * inverse
    hidden_grad = cotangent + inverse * (
        grad_normed
        - jnp.mean(grad_normed, axis=-1, keepdims=True)
        - normed * jnp.mean(grad_normed * normed, axis=-1, keepdims=True)
    )

    stats = a_grad[:, qcols + acols :]
    qb_grad = stats[: heads * (3 * HD // dp), 7].reshape(heads, -1)
    ub_grad = stats[: fcols // dp, 5].reshape(up_bias.shape[0], -1)
    total = stats
    for k in range(1, tensor):
        total = total + zswap(stats, k)
    mine = lax.dynamic_slice_in_dim(total, z_at * part, part, 0)[:, :8].T

    return (
        hidden_out,
        hidden_grad,
        mine[0],
        mine[1],
        mine[2],
        mine[3],
        a_grad[:, :qcols],
        qb_grad,
        a_grad[:, qcols : qcols + acols].T,
        mine[4],
        b_grad[:, :fcols],
        ub_grad,
        b_grad[:, fcols:].T,
        mine[4],
    )


def solution(mesh):
    both = P(("dp", "tensor"))
    wide = P(("dp", "tensor"), None)
    step = jax.shard_map(
        functools.partial(block, dp=mesh.shape["dp"], tensor=mesh.shape["tensor"]),
        mesh=mesh,
        in_specs=(
            wide, P("dp", None), wide, both, both, both, both, P("dp", "tensor"),
            P("tensor", "dp"), P("tensor", "dp"), both, P("dp", "tensor"), P("tensor", "dp"),
            P("tensor", "dp"), both,
        ),
        out_specs=(
            wide, wide, both, both, both, both, P("dp", "tensor"), P("tensor", "dp"),
            P("tensor", "dp"), both, P("dp", "tensor"), P("tensor", "dp"), P("tensor", "dp"), both,
        ),
        check_vma=False,
    )
    if mesh.shape["dp"] != len(EXCHANGE):
        return step
    return step
```

```python
import functools
import math

import jax
import jax.numpy as jnp
from jax import lax
from jax.experimental import pallas as pl
from jax.experimental.pallas import tpu as pltpu
from jax.sharding import PartitionSpec as P


HD = 64
ROT = 16
MAX_DOC = 256
QB = 128
norm_eps = 1e-05

BF = jnp.bfloat16
F32 = jnp.float32


def dot(a, b):
    return lax.dot_general(a, b, (((1,), (0,)), ((), ())), preferred_element_type=F32)


def dot_t(a, b):
    return lax.dot_general(a, b, (((1,), (1,)), ((), ())), preferred_element_type=F32)


def t_dot(a, b):
    return lax.dot_general(a, b, (((0,), (0,)), ((), ())), preferred_element_type=F32)


def vmem(mib):
    return pltpu.CompilerParams(vmem_limit_bytes=mib * 1024 * 1024)


def cost(flops, ins, outs):
    size = sum(a.size * a.dtype.itemsize for a in (*ins, *outs))
    return pl.CostEstimate(flops=int(flops), bytes_accessed=int(size), transcendentals=0)


def whole(shape):
    zeros = (0,) * len(shape)
    return pl.BlockSpec(tuple(shape), lambda i, *_: zeros)


def swap(array, axis, size, bits):
    return lax.ppermute(array, axis, [(i, i ^ bits) for i in range(size)])


def rotate(wide, tables, sign):
    width = wide.shape[-1]
    half = ROT // 2
    lane = lax.broadcasted_iota(jnp.int32, (1, width), 1)
    turns = ((lane // HD) % 3 < 2).astype(F32)
    reps = width // tables.shape[-1]
    cosine, low, high = (jnp.concatenate([tables[j]] * reps, axis=1) * turns for j in range(3))
    down = pltpu.roll(wide, width - half, 1)
    up = pltpu.roll(wide, half, 1)
    return wide + wide * cosine + sign * (down * low + up * high)


EXCHANGE = (0, 2, 4, 6, 1, 3, 5, 7)
SMALL_ROWS = 16
SMALL_LANES = 128


def assemble_body(place, *refs, count, rows, small):
    blocks = refs[:count]
    full = refs[count]
    sems = refs[-1]
    copies = []
    for at, k in enumerate(EXCHANGE):
        start = pl.multiple_of((place[0] ^ k) * rows, 16)
        copies.append(
            pltpu.make_async_copy(
                blocks[at].at[pl.ds(0, rows), :], full.at[pl.ds(start, rows), :], sems.at[at]
            )
        )
        if small:
            copies.append(
                pltpu.make_async_copy(
                    blocks[at].at[pl.ds(rows, SMALL_ROWS), :], refs[-2].at[place[0] ^ k], sems.at[count + at]
                )
            )
    for copy in copies:
        copy.start()
    for copy in copies:
        copy.wait()
    if small:
        gains, qb, ub = refs[count + 1 : count + 4]
        nvec, heads, units = small
        lanes = SMALL_LANES
        qpart, upart = qb.shape[1] // heads // count, ub.shape[1] // units // count
        for d in range(count):
            wide = refs[-2][d].astype(F32)
            vals = wide[:, :lanes] + wide[:, lanes : 2 * lanes] + wide[:, 2 * lanes : 3 * lanes]
            gains[0:nvec, d * rows : (d + 1) * rows] = vals[0:nvec, :rows]
            for h in range(heads):
                at = (h * count + d) * qpart
                qb[:, at : at + qpart] = vals[nvec + h : nvec + h + 1, :qpart]
            for u in range(units):
                at = (u * count + d) * upart
                row = nvec + heads + u
                ub[:, at : at + upart] = vals[row : row + 1, :upart]


def assemble(place, blocks, rows, small):
    count = len(blocks)
    cols = blocks[0].shape[1]
    anywhere = pl.BlockSpec(memory_space=pl.ANY)
    outs = [jax.ShapeDtypeStruct((count * rows, cols), BF)]
    specs = [anywhere]
    scratch = []
    if small:
        nvec, qcols, heads, fcols, units = small
        outs += [
            jax.ShapeDtypeStruct(shape, F32) for shape in ((nvec, count * rows), (1, qcols), (1, fcols))
        ]
        specs += [whole(o.shape) for o in outs[1:]]
        scratch = [pltpu.VMEM((count, SMALL_ROWS, cols), BF)]
        small = (nvec, heads, units)
    return pl.pallas_call(
        functools.partial(assemble_body, count=count, rows=rows, small=small),
        grid_spec=pltpu.PrefetchScalarGridSpec(
            num_scalar_prefetch=1,
            grid=(1,),
            in_specs=[anywhere] * count,
            out_specs=specs,
            scratch_shapes=scratch + [pltpu.SemaphoreType.DMA((2 * count,))],
        ),
        out_shape=outs,
        compiler_params=vmem(4),
    )(place, *blocks)


def prep_body(meta, cot, half_o, sum_o):
    half_o[...] = cot[...].astype(BF)
    sum_o[...] = jnp.broadcast_to(jnp.sum(cot[...], axis=0, keepdims=True), sum_o.shape)


def final_body(meta, own, one, two, hid, cot, out_o):
    x = hid[...].astype(F32)
    cent = x - jnp.mean(x, axis=-1, keepdims=True)
    inverse = lax.rsqrt(jnp.mean(cent * cent, axis=-1, keepdims=True) + norm_eps)
    normed = cent * inverse
    n = own[...].astype(F32) + one[...].astype(F32) + two[...].astype(F32)
    out_o[...] = cot[...] + inverse * (
        n - jnp.mean(n, axis=-1, keepdims=True) - normed * jnp.mean(n * normed, axis=-1, keepdims=True)
    )


def windows(length):
    reach = -(-(MAX_DOC - 1) // QB)
    return [(max(0, i - reach) * QB, (i + 1) * QB) for i in range(length // QB)]


def spot(meta, a, tokens):
    return pl.ds(pl.multiple_of(((meta[0] % 2) ^ a) * tokens, tokens), tokens)


def attn_fwd_body(
    meta, hid_a, hid_b, gains, wa, qb, tables, segc, segr,
    xhat_o, first_o, second_o, mixed_o, att_o, p_o, scratch,
):
    qcols = qb.shape[1]
    tokens = hid_a.shape[0]
    for a, hid in enumerate((hid_a, hid_b)):
        at = spot(meta, a, tokens)
        x = hid[...].astype(F32)
        cent = x - jnp.mean(x, axis=-1, keepdims=True)
        spread = jnp.mean(cent * cent, axis=-1, keepdims=True)
        xhat = cent * lax.rsqrt(spread + norm_eps)
        xhat_o[at, :] = xhat.astype(BF)
        first_o[at, :] = (xhat * gains[0:1, :] + gains[1:2, :]).astype(BF)
        second_o[at, :] = (xhat * gains[2:3, :] + gains[3:4, :]).astype(BF)
    seqs, _, length = segr.shape
    heads = qcols // (3 * HD)
    scratch[...] = jnp.zeros_like(scratch)
    for r in range(seqs):
        row = slice(r * length, (r + 1) * length)
        scratch[:, :qcols] = dot(first_o[row, :], wa[:, :qcols]) + qb[...]
        mixed_o[row, :] = rotate(scratch[...], tables, 1.0).astype(BF)
    for r in range(seqs):
        start = r * length
        for i, (lo, hi) in enumerate(windows(length)):
            width = hi - lo
            qs = slice(start + i * QB, start + (i + 1) * QB)
            ks = slice(start + lo, start + hi)
            rows = lax.broadcasted_iota(jnp.int32, (QB, width), 0) + i * QB
            cols = lax.broadcasted_iota(jnp.int32, (QB, width), 1) + lo
            mask = (segc[qs, :] == segr[r, :, lo:hi]) & (rows >= cols)
            for h in range(heads):
                base = h * 3 * HD
                q = mixed_o[qs, base : base + HD]
                k = mixed_o[ks, base + HD : base + 2 * HD]
                v = mixed_o[ks, base + 2 * HD : base + 3 * HD]
                s = jnp.where(mask, dot_t(q, k) * (HD**-0.5), -1e30)
                p = jnp.exp(s - jnp.max(s, axis=-1, keepdims=True))
                w = (p * (1.0 / jnp.sum(p, axis=-1, keepdims=True))).astype(BF)
                att_o[qs, h * HD : (h + 1) * HD] = dot(w, v).astype(BF)
                p_o[r, h, i, :, :width] = w


def mlp_fwd_body(meta, second, att, wa, wb, ub, active_o, slope_o, *outs, qcols):
    fcols = ub.shape[1]
    tokens = outs[0].shape[0]
    for a in range(2):
        at = spot(meta, a, tokens)
        pre = dot(second[at, :], wb[:, :fcols]) + ub[...]
        cumulative = 0.5 * (1.0 + lax.erf(pre * (1.0 / math.sqrt(2.0))))
        density = jnp.exp(-0.5 * pre * pre) * (1.0 / math.sqrt(2.0 * math.pi))
        act = (pre * cumulative).astype(BF)
        active_o[at, :] = act
        slope_o[at, :] = (cumulative + pre * density).astype(BF)
        outs[a][...] = (dot_t(att[at, :], wa[:, qcols:]) + dot_t(act, wb[:, fcols:])).astype(BF)


def mlp_bwd_body(
    meta, cot_a, cot_b, act, slope, second, xhat, gains, wb, *refs, fcols, blocks, split, chained,
):
    tokens = cot_a.shape[0]
    if chained:
        up_in, down_in, ub_in, stat_in, n_o, keep_o, send_o, ub_o, stat_o, gup, gdown = refs
    else:
        n_o, gup, gdown, ub_o, stat_o = refs
    for a, ref in enumerate((cot_a, cot_b)):
        at = spot(meta, a, tokens)
        c = ref[...]
        down = t_dot(c, act[at, :])
        gp = dot(c, wb[:, fcols:]) * slope[at, :].astype(F32)
        gph = gp.astype(BF)
        up = t_dot(second[at, :], gph)
        part = dot_t(gph, wb[:, :fcols])
        n_o[at, :] = (part * gains[2:3, :]).astype(BF)
        sums = (
            jnp.sum(gp, axis=0, keepdims=True),
            jnp.sum(part * xhat[at, :].astype(F32), axis=0, keepdims=True),
            jnp.sum(part, axis=0, keepdims=True),
        )
        if a:
            gdown[...] += down
            gup[...] += up
            ub_o[0:1, :] += sums[0]
            stat_o[0:1, :] += sums[1]
            stat_o[1:2, :] += sums[2]
        elif chained:
            gdown[...] = down_in[...] + down
            gup[...] = up_in[...] + up
            ub_o[0:1, :] = ub_in[0:1, :] + sums[0]
            stat_o[0:1, :] = stat_in[0:1, :] + sums[1]
            stat_o[1:2, :] = stat_in[1:2, :] + sums[2]
        else:
            gdown[...] = down
            gup[...] = up
            ub_o[0:1, :] = sums[0]
            stat_o[0:1, :] = sums[1]
            stat_o[1:2, :] = sums[2]
    if chained:
        emit(meta, (gup, gdown), keep_o, send_o, blocks, split)


def emit(meta, parts, keep_o, send_o, blocks, split):
    rows = keep_o.shape[1]
    for k in range(blocks):
        if split:
            start = pl.multiple_of((meta[1] ^ k) * rows, 16)
            target = send_o if k % 2 else keep_o
            slot = k // 2
        else:
            start, target, slot = k * rows, keep_o, k
        at = 0
        for part in parts:
            wide = part.shape[1]
            target[slot, :, at : at + wide] = part[pl.ds(start, rows), :].astype(target.dtype)
            at += wide


def attn_bwd_body(
    meta, cot_a, cot_b, mix, p_in, att, first, xhat, n_in, gains, wa, tables,
    n_a, n_b, stat_o, qb_o, gqkv, gdense, dmix, cot, *, heads, qcols, seqs, last,
):
    tokens = cot_a.shape[0]
    for a, ref in enumerate((cot_a, cot_b)):
        cot[spot(meta, a, tokens), :] = ref[...]
    c = cot[...]
    length = c.shape[0] // seqs
    down = t_dot(c, att[...])
    gdense[...] = down if last is None else last[1][...] + down
    ga = dot(c, wa[:, qcols:]).astype(BF)
    dmix[...] = jnp.zeros_like(dmix)
    for r in range(seqs):
        start = r * length
        for h in range(heads):
            base = h * 3 * HD
            for i, (lo, hi) in enumerate(windows(length)):
                width = hi - lo
                qs = slice(start + i * QB, start + (i + 1) * QB)
                ks = slice(start + lo, start + hi)
                q = mix[qs, base : base + HD]
                k = mix[ks, base + HD : base + 2 * HD]
                v = mix[ks, base + 2 * HD : base + 3 * HD]
                g = ga[qs, h * HD : (h + 1) * HD]
                w = p_in[r, h, i, :, :width]
                wide = w.astype(F32)
                gw = dot_t(g, v)
                inner = jnp.sum(wide * gw, axis=-1, keepdims=True)
                ds = (wide * (gw - inner) * (HD**-0.5)).astype(BF)
                dmix[qs, base : base + HD] = dot(ds, k)
                dmix[ks, base + HD : base + 2 * HD] += t_dot(ds, q)
                dmix[ks, base + 2 * HD : base + 3 * HD] += t_dot(w, g)
        row = slice(start, start + length)
        dmix[row, :] = rotate(dmix[row, :], tables, -1.0)
    turned = dmix[...]
    total = jnp.sum(turned, axis=0, keepdims=True)
    qb_o[0:1, :] = total if last is None else last[3][0:1, :] + total
    g = turned[:, :qcols].astype(BF)
    up = t_dot(first[...], g)
    gqkv[...] = up if last is None else last[0][...] + up
    part = dot_t(g, wa[:, :qcols])
    sums = (
        jnp.sum(part * xhat[...].astype(F32), axis=0, keepdims=True),
        jnp.sum(part, axis=0, keepdims=True),
    )
    for j in range(2):
        stat_o[j : j + 1, :] = sums[j] if last is None else last[2][j : j + 1, :] + sums[j]
    cot[...] = (part * gains[0:1, :] + n_in[...].astype(F32)).astype(BF)
    for a, out in enumerate((n_a, n_b)):
        out[...] = cot[spot(meta, a, tokens), :]


def pack_body(
    meta, gqkv, gdense, stat, stat_two, cot_sum, ub, qb, keep_o, send_o, wide, cols,
    *, blocks, split, heads, units,
):
    rows = keep_o.shape[1]
    lanes = cols.shape[1]
    wide[...] = jnp.zeros_like(wide)
    wide[0:2, :] = stat[0:2, :]
    wide[2:4, :] = stat_two[0:2, :]
    wide[4:5, :] = cot_sum[0:1, :]
    cols[...] = wide[...].T
    for lane_at, source, groups, size in ((5, ub, units, ub.shape[1] // units), (7, qb, heads, 3 * HD)):
        per = size // blocks
        tall = jnp.broadcast_to(source[0:1, :], (lanes, source.shape[1])).T
        lane = lax.broadcasted_iota(jnp.int32, (per, lanes), 1)
        for d in range(blocks):
            for g in range(groups):
                at = slice(d * rows + g * per, d * rows + (g + 1) * per)
                src = tall[g * size + d * per : g * size + (d + 1) * per, :]
                cols[at, :] = jnp.where(lane == lane_at, src, cols[at, :])
    emit(meta, (gqkv, gdense, cols), keep_o, send_o, blocks, split)


def gather_weights(shard, rows, place, dp, small=None):
    got = {k: swap(shard, "dp", dp, k) for k in (6, 2, 4)}
    near = [shard] + [got[k] for k in (2, 4, 6)]
    far = [swap(a, "dp", dp, 1) for a in near]
    return assemble(place, near + far, rows, small)


def reduce_weights(keep, send, dp):
    if send is None:
        total = lax.psum_scatter(keep, "dp", scatter_dimension=0, tiled=True)
        return total[0]
    got = swap(send, "dp", dp, 1)
    near = [keep[j].astype(F32) + got[j].astype(F32) for j in range(keep.shape[0])]
    total = near[0]
    for j in (3, 1, 2):
        total = total + swap(near[j].astype(BF), "dp", dp, 2 * j).astype(F32)
    return total


def rotary_tables(length):
    place = jnp.arange(length).astype(F32)[:, None]
    entry = jnp.arange(128) % HD
    half = ROT // 2
    turns = (entry < ROT)[None, :]
    frequency = 1.0 / 10000.0 ** ((entry % half).astype(F32) * 2.0 / ROT)
    angle = place * frequency[None, :]
    cosine = jnp.where(turns, jnp.cos(angle) - 1.0, 0.0)
    sine = jnp.where(turns, jnp.sin(angle), 0.0)
    low = (entry < half)[None, :]
    return jnp.stack([cosine, jnp.where(low, -sine, 0.0), jnp.where(low, 0.0, sine)])


def call(body, out_shape, scratch, *args, mib=16, flops=0):
    return pl.pallas_call(
        body,
        grid_spec=pltpu.PrefetchScalarGridSpec(
            num_scalar_prefetch=1,
            grid=(1,),
            in_specs=[whole(a.shape) for a in args[1:]],
            out_specs=[whole(o.shape) for o in out_shape],
            scratch_shapes=[pltpu.VMEM(shape, dtype) for shape, dtype in scratch],
        ),
        out_shape=out_shape,
        compiler_params=vmem(mib),
        cost_estimate=cost(flops, args[1:], out_shape),
    )(*args)


def block(
    hidden_in, segment_ids, cotangent, norm1_gain, norm1_bias, norm2_gain, norm2_bias,
    qkv_weight, qkv_bias, dense_weight, dense_bias, up_weight, up_bias, down_weight, down_bias,
    *, dp, tensor,
):
    d_at = lax.axis_index("dp")
    z_at = lax.axis_index("tensor")
    meta = jnp.stack([z_at, d_at]).astype(jnp.int32)
    place = d_at.astype(jnp.int32)[None]
    tokens, width = hidden_in.shape
    seqs, length = segment_ids.shape
    hseqs = seqs // 2
    htok = tokens * tensor // 2
    qcols = qkv_weight.shape[1]
    heads = qcols // (3 * HD)
    acols = heads * HD
    fcols = up_weight.shape[1]
    qwide = -(-qcols // 128) * 128
    rows = width // dp
    split = dp == len(EXCHANGE) and rows % 16 == 0
    stat_lanes = 128

    def sds(shape, dtype=F32):
        return jax.ShapeDtypeStruct(shape, dtype)

    def zswap(a, bits):
        return swap(a, "tensor", tensor, bits)

    vecs = jnp.stack([norm1_gain, norm1_bias, norm2_gain, norm2_bias, dense_bias, down_bias])
    nvec, part = vecs.shape
    got = [vecs] + [zswap(vecs, k) for k in range(1, tensor)]
    lanes_of = []
    for t in range(tensor):
        value = got[0]
        for k in range(1, tensor):
            value = jnp.where(z_at == t ^ k, got[k], value)
        lanes_of.append(value)
    units = up_bias.shape[0]

    def lanes(a):
        return jnp.pad(a.astype(F32), ((0, 0), (0, SMALL_LANES - a.shape[1])))

    small = jnp.concatenate(
        [
            lanes(jnp.concatenate(lanes_of, axis=1)), lanes(qkv_bias), lanes(up_bias),
            jnp.zeros((SMALL_ROWS - nvec - heads - units, SMALL_LANES), F32),
        ],
        axis=0,
    )
    high = lax.reduce_precision(small, 8, 7)
    middle = lax.reduce_precision(small - high, 8, 7)
    low = small - high - middle
    triple = jnp.concatenate([high, middle, low], axis=1).astype(BF)

    half_cot, cot_sum = call(prep_body, [sds((tokens, width), BF), sds((8, width))], [], meta, cotangent, mib=4)
    hid_two = zswap(hidden_in, 2)
    hid_one = zswap(hidden_in, 1)
    hid_three = zswap(hid_two, 1)
    cot_two = zswap(half_cot, 2)
    cot_one = zswap(half_cot, 1)
    cot_three = zswap(cot_two, 1)

    acols_all = qcols + acols
    triple = jnp.pad(triple, ((0, 0), (0, acols_all - triple.shape[1])))
    pack_a = jnp.concatenate(
        [jnp.concatenate([qkv_weight, dense_weight.T], axis=1), triple], axis=0
    )
    pack_b = jnp.concatenate([up_weight, down_weight.T], axis=1)
    if split:
        wa, gains, qb, ub = gather_weights(pack_a, rows, place, dp, (nvec, qcols, heads, fcols, units))
        (wb,) = gather_weights(pack_b, rows, place, dp)
    else:
        every = lax.all_gather(pack_a, "dp", axis=0)
        wa = every[:, :rows].reshape(width, acols_all)
        wb = lax.all_gather(pack_b, "dp", axis=0, tiled=True)
        trio = every[:, rows:].astype(F32)
        vals = sum(trio[:, :, j * SMALL_LANES : (j + 1) * SMALL_LANES] for j in range(3))
        gains = vals[:, :nvec, :rows].transpose(1, 0, 2).reshape(nvec, width)
        qb = vals[:, nvec : nvec + heads, : 3 * HD // dp].transpose(1, 0, 2).reshape(1, qcols)
        ub = vals[:, nvec + heads : nvec + heads + units, : fcols // units // dp]
        ub = ub.transpose(1, 0, 2).reshape(1, fcols)
    tables = rotary_tables(length)

    side = z_at // 2
    near_ids = lax.dynamic_slice_in_dim(segment_ids, side * hseqs, hseqs, 0)
    far_ids = lax.dynamic_slice_in_dim(segment_ids, (1 - side) * hseqs, hseqs, 0)
    nwin = length // QB
    wwin = max(hi - lo for lo, hi in windows(length))

    def forward(hid_a, hid_b, ids):
        fa = call(
            attn_fwd_body,
            [
                sds((htok, width), BF), sds((htok, width), BF), sds((htok, width), BF),
                sds((htok, qwide), BF), sds((htok, acols), BF), sds((hseqs, heads, nwin, QB, wwin), BF),
            ],
            [((htok, qwide), F32)],
            meta, hid_a, hid_b, gains, wa, qb, tables, ids.reshape(htok, 1),
            ids.reshape(hseqs, 1, length), flops=7e9,
        )
        xhat, first, second, mixed, att, weights = fa
        active, slope, out_a, out_b = call(
            functools.partial(mlp_fwd_body, qcols=qcols),
            [
                sds((htok, fcols), BF), sds((htok, fcols), BF), sds((tokens, width), BF),
                sds((tokens, width), BF),
            ],
            [], meta, second, att, wa, wb, ub, flops=3e9,
        )
        return dict(
            xhat=xhat, first=first, second=second, mixed=mixed, att=att, weights=weights,
            active=active, slope=slope, out=(out_a, out_b),
        )

    near = forward(hidden_in, hid_one, near_ids)
    far = forward(hid_two, hid_three, far_ids)

    def scatter(near_parts, far_parts):
        relay = zswap(far_parts[1], 1)
        pair = (far_parts[0].astype(F32) + relay.astype(F32)).astype(BF)
        two = zswap(pair, 2)
        one = zswap(near_parts[1], 1)
        return near_parts[0], one, two

    branch = sum(a.astype(F32) for a in scatter(near["out"], far["out"]))
    hidden_out = hidden_in.astype(F32) + branch + gains[4] + gains[5]

    if split:
        half_blocks = (dp // 2, rows)
    else:
        half_blocks = (dp, rows)

    def grad_shapes(cols):
        return [sds(half_blocks + (cols,)), sds(half_blocks + (cols,) if split else (1, 16, 128), BF)]

    def mlp_bwd(cot_a, cot_b, kept, before):
        sums = [sds((8, fcols)), sds((8, width))]
        grads = [sds((width, fcols)), sds((width, fcols))]
        chained = before is not None
        return call(
            functools.partial(mlp_bwd_body, fcols=fcols, blocks=dp, split=split, chained=chained),
            [sds((htok, width), BF)] + (grad_shapes(2 * fcols) + sums if chained else grads + sums),
            [((width, fcols), F32)] * 2 if chained else [],
            meta, cot_a, cot_b, *(kept[k] for k in ("active", "slope", "second", "xhat")), gains, wb,
            *(before if chained else ()), flops=5e9,
        )

    n_two_far, *sums_far = mlp_bwd(cot_two, cot_three, far, None)
    n_two_near, b_keep, b_send, ub_sum, stat_two = mlp_bwd(half_cot, cot_one, near, sums_far)

    def attn_bwd(cot_a, cot_b, kept, n_half, before):
        fixed = 12

        def body(*refs):
            ins = refs[:fixed]
            last = None if before is None else (refs[fixed], refs[fixed + 1], refs[fixed + 2], refs[fixed + 3])
            outs = refs[fixed + (0 if before is None else 4) :]
            attn_bwd_body(*ins, *outs, heads=heads, qcols=qcols, seqs=hseqs, last=last)

        return call(
            body,
            [
                sds((tokens, width), BF), sds((tokens, width), BF), sds((8, width)), sds((8, qwide)),
                sds((width, qcols)), sds((width, acols)),
            ],
            [((htok, qwide), F32), ((htok, width), BF)],
            meta, cot_a, cot_b, kept["mixed"], kept["weights"], kept["att"], kept["first"], kept["xhat"],
            n_half, gains, wa, tables, *(() if before is None else before), flops=9e9,
        )

    *n_far, s_far, q_far, gqkv_far, gdense_far = attn_bwd(cot_two, cot_three, far, n_two_far, None)
    *n_near, stat_one, qb_sum, gqkv, gdense = attn_bwd(
        half_cot, cot_one, near, n_two_near, (gqkv_far, gdense_far, s_far, q_far)
    )
    a_keep, a_send = call(
        functools.partial(pack_body, blocks=dp, split=split, heads=heads, units=units),
        grad_shapes(qcols + acols + stat_lanes),
        [((stat_lanes, width), F32), ((width, stat_lanes), F32)],
        meta, gqkv, gdense, stat_one, stat_two, cot_sum, ub_sum, qb_sum, flops=1e9,
    )

    b_grad = reduce_weights(b_keep, b_send if split else None, dp)
    grad_parts = scatter(n_near, n_far)
    a_grad = reduce_weights(a_keep, a_send if split else None, dp)
    (hidden_grad,) = call(
        final_body, [sds((tokens, width))], [], meta, *grad_parts, hidden_in, cotangent, mib=8, flops=2e9
    )

    stats = a_grad[:, qcols + acols :]
    qb_grad = stats[: heads * (3 * HD // dp), 7].reshape(heads, -1)
    ub_grad = stats[: fcols // dp, 5].reshape(up_bias.shape[0], -1)
    total = stats
    for k in range(1, tensor):
        total = total + zswap(stats, k)
    mine = lax.dynamic_slice_in_dim(total, z_at * part, part, 0)[:, :8].T

    return (
        hidden_out,
        hidden_grad,
        mine[0],
        mine[1],
        mine[2],
        mine[3],
        a_grad[:, :qcols],
        qb_grad,
        a_grad[:, qcols : qcols + acols].T,
        mine[4],
        b_grad[:, :fcols],
        ub_grad,
        b_grad[:, fcols:].T,
        mine[4],
    )


def solution(mesh):
    both = P(("dp", "tensor"))
    wide = P(("dp", "tensor"), None)
    step = jax.shard_map(
        functools.partial(block, dp=mesh.shape["dp"], tensor=mesh.shape["tensor"]),
        mesh=mesh,
        in_specs=(
            wide, P("dp", None), wide, both, both, both, both, P("dp", "tensor"),
            P("tensor", "dp"), P("tensor", "dp"), both, P("dp", "tensor"), P("tensor", "dp"),
            P("tensor", "dp"), both,
        ),
        out_specs=(
            wide, wide, both, both, both, both, P("dp", "tensor"), P("tensor", "dp"),
            P("tensor", "dp"), both, P("dp", "tensor"), P("tensor", "dp"), P("tensor", "dp"), both,
        ),
        check_vma=False,
    )
    if mesh.shape["dp"] != len(EXCHANGE):
        return step
    return step
```

```python
import functools
import math

import jax
import jax.numpy as jnp
from jax import lax
from jax.experimental import pallas as pl
from jax.experimental.pallas import tpu as pltpu
from jax.sharding import PartitionSpec as P


HD = 64
ROT = 16
MAX_DOC = 256
QB = 128
norm_eps = 1e-05

BF = jnp.bfloat16
F32 = jnp.float32


def dot(a, b):
    return lax.dot_general(a, b, (((1,), (0,)), ((), ())), preferred_element_type=F32)


def dot_t(a, b):
    return lax.dot_general(a, b, (((1,), (1,)), ((), ())), preferred_element_type=F32)


def t_dot(a, b):
    return lax.dot_general(a, b, (((0,), (0,)), ((), ())), preferred_element_type=F32)


def vmem(mib):
    return pltpu.CompilerParams(vmem_limit_bytes=mib * 1024 * 1024)


def cost(flops, ins, outs):
    size = sum(a.size * a.dtype.itemsize for a in (*ins, *outs))
    return pl.CostEstimate(flops=int(flops), bytes_accessed=int(size), transcendentals=0)


def whole(shape):
    zeros = (0,) * len(shape)
    return pl.BlockSpec(tuple(shape), lambda i, *_: zeros)


def swap(array, axis, size, bits):
    return lax.ppermute(array, axis, [(i, i ^ bits) for i in range(size)])


def rotate(wide, tables, sign):
    width = wide.shape[-1]
    half = ROT // 2
    lane = lax.broadcasted_iota(jnp.int32, (1, width), 1)
    turns = ((lane // HD) % 3 < 2).astype(F32)
    reps = width // tables.shape[-1]
    cosine, low, high = (jnp.concatenate([tables[j]] * reps, axis=1) * turns for j in range(3))
    down = pltpu.roll(wide, width - half, 1)
    up = pltpu.roll(wide, half, 1)
    return wide + wide * cosine + sign * (down * low + up * high)


EXCHANGE = (0, 2, 4, 6, 1, 3, 5, 7)
SMALL_ROWS = 16
SMALL_LANES = 128


def assemble_body(place, *refs, count, rows, small):
    blocks = refs[:count]
    full = refs[count]
    sems = refs[-1]
    copies = []
    for at, k in enumerate(EXCHANGE):
        start = pl.multiple_of((place[0] ^ k) * rows, 16)
        copies.append(
            pltpu.make_async_copy(
                blocks[at].at[pl.ds(0, rows), :], full.at[pl.ds(start, rows), :], sems.at[at]
            )
        )
        if small:
            copies.append(
                pltpu.make_async_copy(
                    blocks[at].at[pl.ds(rows, SMALL_ROWS), :], refs[-2].at[place[0] ^ k], sems.at[count + at]
                )
            )
    for copy in copies:
        copy.start()
    for copy in copies:
        copy.wait()
    if small:
        gains, qb, ub = refs[count + 1 : count + 4]
        nvec, heads, units = small
        lanes = SMALL_LANES
        qpart, upart = qb.shape[1] // heads // count, ub.shape[1] // units // count
        for d in range(count):
            wide = refs[-2][d].astype(F32)
            vals = wide[:, :lanes] + wide[:, lanes : 2 * lanes] + wide[:, 2 * lanes : 3 * lanes]
            gains[0:nvec, d * rows : (d + 1) * rows] = vals[0:nvec, :rows]
            for h in range(heads):
                at = (h * count + d) * qpart
                qb[:, at : at + qpart] = vals[nvec + h : nvec + h + 1, :qpart]
            for u in range(units):
                at = (u * count + d) * upart
                row = nvec + heads + u
                ub[:, at : at + upart] = vals[row : row + 1, :upart]


def assemble(place, blocks, rows, small):
    count = len(blocks)
    cols = blocks[0].shape[1]
    anywhere = pl.BlockSpec(memory_space=pl.ANY)
    outs = [jax.ShapeDtypeStruct((count * rows, cols), BF)]
    specs = [anywhere]
    scratch = []
    if small:
        nvec, qcols, heads, fcols, units = small
        outs += [
            jax.ShapeDtypeStruct(shape, F32) for shape in ((nvec, count * rows), (1, qcols), (1, fcols))
        ]
        specs += [whole(o.shape) for o in outs[1:]]
        scratch = [pltpu.VMEM((count, SMALL_ROWS, cols), BF)]
        small = (nvec, heads, units)
    return pl.pallas_call(
        functools.partial(assemble_body, count=count, rows=rows, small=small),
        grid_spec=pltpu.PrefetchScalarGridSpec(
            num_scalar_prefetch=1,
            grid=(1,),
            in_specs=[anywhere] * count,
            out_specs=specs,
            scratch_shapes=scratch + [pltpu.SemaphoreType.DMA((2 * count,))],
        ),
        out_shape=outs,
        compiler_params=vmem(4),
    )(place, *blocks)


def prep_body(meta, cot, half_o, sum_o):
    half_o[...] = cot[...].astype(BF)
    sum_o[...] = jnp.broadcast_to(jnp.sum(cot[...], axis=0, keepdims=True), sum_o.shape)


def final_body(meta, own, one, two, hid, cot, out_o):
    x = hid[...].astype(F32)
    cent = x - jnp.mean(x, axis=-1, keepdims=True)
    inverse = lax.rsqrt(jnp.mean(cent * cent, axis=-1, keepdims=True) + norm_eps)
    normed = cent * inverse
    n = own[...].astype(F32) + one[...].astype(F32) + two[...].astype(F32)
    out_o[...] = cot[...] + inverse * (
        n - jnp.mean(n, axis=-1, keepdims=True) - normed * jnp.mean(n * normed, axis=-1, keepdims=True)
    )


def windows(length):
    reach = -(-(MAX_DOC - 1) // QB)
    return [(max(0, i - reach) * QB, (i + 1) * QB) for i in range(length // QB)]


def spot(meta, a, tokens):
    return pl.ds(pl.multiple_of(((meta[0] % 2) ^ a) * tokens, tokens), tokens)


def attn_fwd_body(
    meta, hid_a, hid_b, gains, wa, qb, tables, segc, segr,
    xhat_o, first_o, second_o, mixed_o, att_o, p_o, scratch,
):
    qcols = qb.shape[1]
    tokens = hid_a.shape[0]
    for a, hid in enumerate((hid_a, hid_b)):
        at = spot(meta, a, tokens)
        x = hid[...].astype(F32)
        cent = x - jnp.mean(x, axis=-1, keepdims=True)
        spread = jnp.mean(cent * cent, axis=-1, keepdims=True)
        xhat = cent * lax.rsqrt(spread + norm_eps)
        xhat_o[at, :] = xhat.astype(BF)
        first_o[at, :] = (xhat * gains[0:1, :] + gains[1:2, :]).astype(BF)
        second_o[at, :] = (xhat * gains[2:3, :] + gains[3:4, :]).astype(BF)
    seqs, _, length = segr.shape
    heads = qcols // (3 * HD)
    scratch[...] = jnp.zeros_like(scratch)
    for r in range(seqs):
        row = slice(r * length, (r + 1) * length)
        scratch[:, :qcols] = dot(first_o[row, :], wa[:, :qcols]) + qb[...]
        mixed_o[row, :] = rotate(scratch[...], tables, 1.0).astype(BF)
    for r in range(seqs):
        start = r * length
        for i, (lo, hi) in enumerate(windows(length)):
            width = hi - lo
            qs = slice(start + i * QB, start + (i + 1) * QB)
            ks = slice(start + lo, start + hi)
            rows = lax.broadcasted_iota(jnp.int32, (QB, width), 0) + i * QB
            cols = lax.broadcasted_iota(jnp.int32, (QB, width), 1) + lo
            mask = (segc[qs, :] == segr[r, :, lo:hi]) & (rows >= cols)
            for h in range(heads):
                base = h * 3 * HD
                q = mixed_o[qs, base : base + HD]
                k = mixed_o[ks, base + HD : base + 2 * HD]
                v = mixed_o[ks, base + 2 * HD : base + 3 * HD]
                s = jnp.where(mask, dot_t(q, k) * (HD**-0.5), -1e30)
                p = jnp.exp(s - jnp.max(s, axis=-1, keepdims=True))
                w = (p * (1.0 / jnp.sum(p, axis=-1, keepdims=True))).astype(BF)
                att_o[qs, h * HD : (h + 1) * HD] = dot(w, v).astype(BF)
                p_o[r, h, i, :, :width] = w


def mlp_fwd_body(meta, second, att, wa, wb, ub, active_o, slope_o, out_a, out_b, both, *, qcols):
    fcols = ub.shape[1]
    tokens = out_a.shape[0]

    @pl.loop(0, 2)
    def _(i):
        at = pl.ds(pl.multiple_of(i * tokens, tokens), tokens)
        pre = dot(second[at, :], wb[:, :fcols]) + ub[...]
        cumulative = 0.5 * (1.0 + lax.erf(pre * (1.0 / math.sqrt(2.0))))
        density = jnp.exp(-0.5 * pre * pre) * (1.0 / math.sqrt(2.0 * math.pi))
        act = (pre * cumulative).astype(BF)
        active_o[at, :] = act
        slope_o[at, :] = (cumulative + pre * density).astype(BF)
        both[at, :] = (dot_t(att[at, :], wa[:, qcols:]) + dot_t(act, wb[:, fcols:])).astype(BF)

    out_a[...] = both[spot(meta, 0, tokens), :]
    out_b[...] = both[spot(meta, 1, tokens), :]


def mlp_bwd_body(
    meta, cot_a, cot_b, act, slope, second, xhat, gains, wb, *refs, fcols, blocks, split, chained,
):
    tokens = cot_a.shape[0]
    if chained:
        up_in, down_in, ub_in, stat_in, n_o, keep_o, send_o, ub_o, stat_o, gup, gdown = refs
    else:
        n_o, gup, gdown, ub_o, stat_o = refs
    for a, ref in enumerate((cot_a, cot_b)):
        at = spot(meta, a, tokens)
        c = ref[...]
        down = t_dot(c, act[at, :])
        gp = dot(c, wb[:, fcols:]) * slope[at, :].astype(F32)
        gph = gp.astype(BF)
        up = t_dot(second[at, :], gph)
        part = dot_t(gph, wb[:, :fcols])
        n_o[at, :] = (part * gains[2:3, :]).astype(BF)
        sums = (
            jnp.sum(gp, axis=0, keepdims=True),
            jnp.sum(part * xhat[at, :].astype(F32), axis=0, keepdims=True),
            jnp.sum(part, axis=0, keepdims=True),
        )
        if a:
            gdown[...] += down
            gup[...] += up
            ub_o[0:1, :] += sums[0]
            stat_o[0:1, :] += sums[1]
            stat_o[1:2, :] += sums[2]
        elif chained:
            gdown[...] = down_in[...] + down
            gup[...] = up_in[...] + up
            ub_o[0:1, :] = ub_in[0:1, :] + sums[0]
            stat_o[0:1, :] = stat_in[0:1, :] + sums[1]
            stat_o[1:2, :] = stat_in[1:2, :] + sums[2]
        else:
            gdown[...] = down
            gup[...] = up
            ub_o[0:1, :] = sums[0]
            stat_o[0:1, :] = sums[1]
            stat_o[1:2, :] = sums[2]
    if chained:
        emit(meta, (gup, gdown), keep_o, send_o, blocks, split)


def emit(meta, parts, keep_o, send_o, blocks, split):
    rows = keep_o.shape[1]
    for k in range(blocks):
        if split:
            start = pl.multiple_of((meta[1] ^ k) * rows, 16)
            target = send_o if k % 2 else keep_o
            slot = k // 2
        else:
            start, target, slot = k * rows, keep_o, k
        at = 0
        for part in parts:
            wide = part.shape[1]
            target[slot, :, at : at + wide] = part[pl.ds(start, rows), :].astype(target.dtype)
            at += wide


def attn_bwd_body(
    meta, cot_a, cot_b, mix, p_in, att, first, xhat, n_in, gains, wa, tables,
    n_a, n_b, stat_o, qb_o, gqkv, gdense, dmix, cot, *, heads, qcols, seqs, last,
):
    tokens = cot_a.shape[0]
    for a, ref in enumerate((cot_a, cot_b)):
        cot[spot(meta, a, tokens), :] = ref[...]
    c = cot[...]
    length = c.shape[0] // seqs
    down = t_dot(c, att[...])
    gdense[...] = down if last is None else last[1][...] + down
    ga = dot(c, wa[:, qcols:]).astype(BF)
    dmix[...] = jnp.zeros_like(dmix)
    for r in range(seqs):
        start = r * length
        for h in range(heads):
            base = h * 3 * HD
            for i, (lo, hi) in enumerate(windows(length)):
                width = hi - lo
                qs = slice(start + i * QB, start + (i + 1) * QB)
                ks = slice(start + lo, start + hi)
                q = mix[qs, base : base + HD]
                k = mix[ks, base + HD : base + 2 * HD]
                v = mix[ks, base + 2 * HD : base + 3 * HD]
                g = ga[qs, h * HD : (h + 1) * HD]
                w = p_in[r, h, i, :, :width]
                wide = w.astype(F32)
                gw = dot_t(g, v)
                inner = jnp.sum(wide * gw, axis=-1, keepdims=True)
                ds = (wide * (gw - inner) * (HD**-0.5)).astype(BF)
                dmix[qs, base : base + HD] = dot(ds, k)
                dmix[ks, base + HD : base + 2 * HD] += t_dot(ds, q)
                dmix[ks, base + 2 * HD : base + 3 * HD] += t_dot(w, g)
        row = slice(start, start + length)
        dmix[row, :] = rotate(dmix[row, :], tables, -1.0)
    turned = dmix[...]
    total = jnp.sum(turned, axis=0, keepdims=True)
    qb_o[0:1, :] = total if last is None else last[3][0:1, :] + total
    g = turned[:, :qcols].astype(BF)
    up = t_dot(first[...], g)
    gqkv[...] = up if last is None else last[0][...] + up
    part = dot_t(g, wa[:, :qcols])
    sums = (
        jnp.sum(part * xhat[...].astype(F32), axis=0, keepdims=True),
        jnp.sum(part, axis=0, keepdims=True),
    )
    for j in range(2):
        stat_o[j : j + 1, :] = sums[j] if last is None else last[2][j : j + 1, :] + sums[j]
    cot[...] = (part * gains[0:1, :] + n_in[...].astype(F32)).astype(BF)
    for a, out in enumerate((n_a, n_b)):
        out[...] = cot[spot(meta, a, tokens), :]


def pack_body(
    meta, gqkv, gdense, stat, stat_two, cot_sum, ub, qb, keep_o, send_o, wide, cols,
    *, blocks, split, heads, units,
):
    rows = keep_o.shape[1]
    lanes = cols.shape[1]
    wide[...] = jnp.zeros_like(wide)
    wide[0:2, :] = stat[0:2, :]
    wide[2:4, :] = stat_two[0:2, :]
    wide[4:5, :] = cot_sum[0:1, :]
    cols[...] = wide[...].T
    for lane_at, source, groups, size in ((5, ub, units, ub.shape[1] // units), (7, qb, heads, 3 * HD)):
        per = size // blocks
        tall = jnp.broadcast_to(source[0:1, :], (lanes, source.shape[1])).T
        lane = lax.broadcasted_iota(jnp.int32, (per, lanes), 1)
        for d in range(blocks):
            for g in range(groups):
                at = slice(d * rows + g * per, d * rows + (g + 1) * per)
                src = tall[g * size + d * per : g * size + (d + 1) * per, :]
                cols[at, :] = jnp.where(lane == lane_at, src, cols[at, :])
    emit(meta, (gqkv, gdense, cols), keep_o, send_o, blocks, split)


def gather_weights(shard, rows, place, dp, small=None):
    got = {k: swap(shard, "dp", dp, k) for k in (6, 2, 4)}
    near = [shard] + [got[k] for k in (2, 4, 6)]
    far = [swap(a, "dp", dp, 1) for a in near]
    return assemble(place, near + far, rows, small)


def reduce_weights(keep, send, dp):
    if send is None:
        total = lax.psum_scatter(keep, "dp", scatter_dimension=0, tiled=True)
        return total[0]
    got = swap(send, "dp", dp, 1)
    near = [keep[j].astype(F32) + got[j].astype(F32) for j in range(keep.shape[0])]
    total = near[0]
    for j in (3, 1, 2):
        total = total + swap(near[j].astype(BF), "dp", dp, 2 * j).astype(F32)
    return total


def rotary_tables(length):
    place = jnp.arange(length).astype(F32)[:, None]
    entry = jnp.arange(128) % HD
    half = ROT // 2
    turns = (entry < ROT)[None, :]
    frequency = 1.0 / 10000.0 ** ((entry % half).astype(F32) * 2.0 / ROT)
    angle = place * frequency[None, :]
    cosine = jnp.where(turns, jnp.cos(angle) - 1.0, 0.0)
    sine = jnp.where(turns, jnp.sin(angle), 0.0)
    low = (entry < half)[None, :]
    return jnp.stack([cosine, jnp.where(low, -sine, 0.0), jnp.where(low, 0.0, sine)])


def call(body, out_shape, scratch, *args, mib=16, flops=0):
    return pl.pallas_call(
        body,
        grid_spec=pltpu.PrefetchScalarGridSpec(
            num_scalar_prefetch=1,
            grid=(1,),
            in_specs=[whole(a.shape) for a in args[1:]],
            out_specs=[whole(o.shape) for o in out_shape],
            scratch_shapes=[pltpu.VMEM(shape, dtype) for shape, dtype in scratch],
        ),
        out_shape=out_shape,
        compiler_params=vmem(mib),
        cost_estimate=cost(flops, args[1:], out_shape),
    )(*args)


def block(
    hidden_in, segment_ids, cotangent, norm1_gain, norm1_bias, norm2_gain, norm2_bias,
    qkv_weight, qkv_bias, dense_weight, dense_bias, up_weight, up_bias, down_weight, down_bias,
    *, dp, tensor,
):
    d_at = lax.axis_index("dp")
    z_at = lax.axis_index("tensor")
    meta = jnp.stack([z_at, d_at]).astype(jnp.int32)
    place = d_at.astype(jnp.int32)[None]
    tokens, width = hidden_in.shape
    seqs, length = segment_ids.shape
    hseqs = seqs // 2
    htok = tokens * tensor // 2
    qcols = qkv_weight.shape[1]
    heads = qcols // (3 * HD)
    acols = heads * HD
    fcols = up_weight.shape[1]
    qwide = -(-qcols // 128) * 128
    rows = width // dp
    split = dp == len(EXCHANGE) and rows % 16 == 0
    stat_lanes = 128

    def sds(shape, dtype=F32):
        return jax.ShapeDtypeStruct(shape, dtype)

    def zswap(a, bits):
        return swap(a, "tensor", tensor, bits)

    vecs = jnp.stack([norm1_gain, norm1_bias, norm2_gain, norm2_bias, dense_bias, down_bias])
    nvec, part = vecs.shape
    got = [vecs] + [zswap(vecs, k) for k in range(1, tensor)]
    lanes_of = []
    for t in range(tensor):
        value = got[0]
        for k in range(1, tensor):
            value = jnp.where(z_at == t ^ k, got[k], value)
        lanes_of.append(value)
    units = up_bias.shape[0]

    def lanes(a):
        return jnp.pad(a.astype(F32), ((0, 0), (0, SMALL_LANES - a.shape[1])))

    small = jnp.concatenate(
        [
            lanes(jnp.concatenate(lanes_of, axis=1)), lanes(qkv_bias), lanes(up_bias),
            jnp.zeros((SMALL_ROWS - nvec - heads - units, SMALL_LANES), F32),
        ],
        axis=0,
    )
    high = lax.reduce_precision(small, 8, 7)
    middle = lax.reduce_precision(small - high, 8, 7)
    low = small - high - middle
    triple = jnp.concatenate([high, middle, low], axis=1).astype(BF)

    half_cot, cot_sum = call(prep_body, [sds((tokens, width), BF), sds((8, width))], [], meta, cotangent, mib=4)
    hid_two = zswap(hidden_in, 2)
    hid_one = zswap(hidden_in, 1)
    hid_three = zswap(hid_two, 1)
    cot_two = zswap(half_cot, 2)
    cot_one = zswap(half_cot, 1)
    cot_three = zswap(cot_two, 1)

    acols_all = qcols + acols
    triple = jnp.pad(triple, ((0, 0), (0, acols_all - triple.shape[1])))
    pack_a = jnp.concatenate(
        [jnp.concatenate([qkv_weight, dense_weight.T], axis=1), triple], axis=0
    )
    pack_b = jnp.concatenate([up_weight, down_weight.T], axis=1)
    if split:
        wa, gains, qb, ub = gather_weights(pack_a, rows, place, dp, (nvec, qcols, heads, fcols, units))
        (wb,) = gather_weights(pack_b, rows, place, dp)
    else:
        every = lax.all_gather(pack_a, "dp", axis=0)
        wa = every[:, :rows].reshape(width, acols_all)
        wb = lax.all_gather(pack_b, "dp", axis=0, tiled=True)
        trio = every[:, rows:].astype(F32)
        vals = sum(trio[:, :, j * SMALL_LANES : (j + 1) * SMALL_LANES] for j in range(3))
        gains = vals[:, :nvec, :rows].transpose(1, 0, 2).reshape(nvec, width)
        qb = vals[:, nvec : nvec + heads, : 3 * HD // dp].transpose(1, 0, 2).reshape(1, qcols)
        ub = vals[:, nvec + heads : nvec + heads + units, : fcols // units // dp]
        ub = ub.transpose(1, 0, 2).reshape(1, fcols)
    tables = rotary_tables(length)

    side = z_at // 2
    near_ids = lax.dynamic_slice_in_dim(segment_ids, side * hseqs, hseqs, 0)
    far_ids = lax.dynamic_slice_in_dim(segment_ids, (1 - side) * hseqs, hseqs, 0)
    nwin = length // QB
    wwin = max(hi - lo for lo, hi in windows(length))

    def forward(hid_a, hid_b, ids):
        fa = call(
            attn_fwd_body,
            [
                sds((htok, width), BF), sds((htok, width), BF), sds((htok, width), BF),
                sds((htok, qwide), BF), sds((htok, acols), BF), sds((hseqs, heads, nwin, QB, wwin), BF),
            ],
            [((htok, qwide), F32)],
            meta, hid_a, hid_b, gains, wa, qb, tables, ids.reshape(htok, 1),
            ids.reshape(hseqs, 1, length), flops=7e9,
        )
        xhat, first, second, mixed, att, weights = fa
        active, slope, out_a, out_b = call(
            functools.partial(mlp_fwd_body, qcols=qcols),
            [
                sds((htok, fcols), BF), sds((htok, fcols), BF), sds((tokens, width), BF),
                sds((tokens, width), BF),
            ],
            [((htok, width), BF)], meta, second, att, wa, wb, ub, flops=3e9,
        )
        return dict(
            xhat=xhat, first=first, second=second, mixed=mixed, att=att, weights=weights,
            active=active, slope=slope, out=(out_a, out_b),
        )

    near = forward(hidden_in, hid_one, near_ids)
    far = forward(hid_two, hid_three, far_ids)

    def scatter(near_parts, far_parts):
        relay = zswap(far_parts[1], 1)
        pair = (far_parts[0].astype(F32) + relay.astype(F32)).astype(BF)
        two = zswap(pair, 2)
        one = zswap(near_parts[1], 1)
        return near_parts[0], one, two

    branch = sum(a.astype(F32) for a in scatter(near["out"], far["out"]))
    hidden_out = hidden_in.astype(F32) + branch + gains[4] + gains[5]

    if split:
        half_blocks = (dp // 2, rows)
    else:
        half_blocks = (dp, rows)

    def grad_shapes(cols):
        return [sds(half_blocks + (cols,)), sds(half_blocks + (cols,) if split else (1, 16, 128), BF)]

    def mlp_bwd(cot_a, cot_b, kept, before):
        sums = [sds((8, fcols)), sds((8, width))]
        grads = [sds((width, fcols)), sds((width, fcols))]
        chained = before is not None
        return call(
            functools.partial(mlp_bwd_body, fcols=fcols, blocks=dp, split=split, chained=chained),
            [sds((htok, width), BF)] + (grad_shapes(2 * fcols) + sums if chained else grads + sums),
            [((width, fcols), F32)] * 2 if chained else [],
            meta, cot_a, cot_b, *(kept[k] for k in ("active", "slope", "second", "xhat")), gains, wb,
            *(before if chained else ()), flops=5e9,
        )

    n_two_far, *sums_far = mlp_bwd(cot_two, cot_three, far, None)
    n_two_near, b_keep, b_send, ub_sum, stat_two = mlp_bwd(half_cot, cot_one, near, sums_far)

    def attn_bwd(cot_a, cot_b, kept, n_half, before):
        fixed = 12

        def body(*refs):
            ins = refs[:fixed]
            last = None if before is None else (refs[fixed], refs[fixed + 1], refs[fixed + 2], refs[fixed + 3])
            outs = refs[fixed + (0 if before is None else 4) :]
            attn_bwd_body(*ins, *outs, heads=heads, qcols=qcols, seqs=hseqs, last=last)

        return call(
            body,
            [
                sds((tokens, width), BF), sds((tokens, width), BF), sds((8, width)), sds((8, qwide)),
                sds((width, qcols)), sds((width, acols)),
            ],
            [((htok, qwide), F32), ((htok, width), BF)],
            meta, cot_a, cot_b, kept["mixed"], kept["weights"], kept["att"], kept["first"], kept["xhat"],
            n_half, gains, wa, tables, *(() if before is None else before), flops=9e9,
        )

    *n_far, s_far, q_far, gqkv_far, gdense_far = attn_bwd(cot_two, cot_three, far, n_two_far, None)
    *n_near, stat_one, qb_sum, gqkv, gdense = attn_bwd(
        half_cot, cot_one, near, n_two_near, (gqkv_far, gdense_far, s_far, q_far)
    )
    a_keep, a_send = call(
        functools.partial(pack_body, blocks=dp, split=split, heads=heads, units=units),
        grad_shapes(qcols + acols + stat_lanes),
        [((stat_lanes, width), F32), ((width, stat_lanes), F32)],
        meta, gqkv, gdense, stat_one, stat_two, cot_sum, ub_sum, qb_sum, flops=1e9,
    )

    b_grad = reduce_weights(b_keep, b_send if split else None, dp)
    grad_parts = scatter(n_near, n_far)
    a_grad = reduce_weights(a_keep, a_send if split else None, dp)
    (hidden_grad,) = call(
        final_body, [sds((tokens, width))], [], meta, *grad_parts, hidden_in, cotangent, mib=8, flops=2e9
    )

    stats = a_grad[:, qcols + acols :]
    qb_grad = stats[: heads * (3 * HD // dp), 7].reshape(heads, -1)
    ub_grad = stats[: fcols // dp, 5].reshape(up_bias.shape[0], -1)
    total = stats
    for k in range(1, tensor):
        total = total + zswap(stats, k)
    mine = lax.dynamic_slice_in_dim(total, z_at * part, part, 0)[:, :8].T

    return (
        hidden_out,
        hidden_grad,
        mine[0],
        mine[1],
        mine[2],
        mine[3],
        a_grad[:, :qcols],
        qb_grad,
        a_grad[:, qcols : qcols + acols].T,
        mine[4],
        b_grad[:, :fcols],
        ub_grad,
        b_grad[:, fcols:].T,
        mine[4],
    )


def solution(mesh):
    both = P(("dp", "tensor"))
    wide = P(("dp", "tensor"), None)
    step = jax.shard_map(
        functools.partial(block, dp=mesh.shape["dp"], tensor=mesh.shape["tensor"]),
        mesh=mesh,
        in_specs=(
            wide, P("dp", None), wide, both, both, both, both, P("dp", "tensor"),
            P("tensor", "dp"), P("tensor", "dp"), both, P("dp", "tensor"), P("tensor", "dp"),
            P("tensor", "dp"), both,
        ),
        out_specs=(
            wide, wide, both, both, both, both, P("dp", "tensor"), P("tensor", "dp"),
            P("tensor", "dp"), both, P("dp", "tensor"), P("tensor", "dp"), P("tensor", "dp"), both,
        ),
        check_vma=False,
    )
    if mesh.shape["dp"] != len(EXCHANGE):
        return step
    return step
```

```python
import functools
import math

import jax
import jax.numpy as jnp
from jax import lax
from jax.experimental import pallas as pl
from jax.experimental.pallas import tpu as pltpu
from jax.sharding import PartitionSpec as P


HD = 64
ROT = 16
MAX_DOC = 256
QB = 128
norm_eps = 1e-05

BF = jnp.bfloat16
F32 = jnp.float32


def dot(a, b):
    return lax.dot_general(a, b, (((1,), (0,)), ((), ())), preferred_element_type=F32)


def dot_t(a, b):
    return lax.dot_general(a, b, (((1,), (1,)), ((), ())), preferred_element_type=F32)


def t_dot(a, b):
    return lax.dot_general(a, b, (((0,), (0,)), ((), ())), preferred_element_type=F32)


def vmem(mib):
    return pltpu.CompilerParams(vmem_limit_bytes=mib * 1024 * 1024)


def cost(flops, ins, outs):
    size = sum(a.size * a.dtype.itemsize for a in (*ins, *outs))
    return pl.CostEstimate(flops=int(flops), bytes_accessed=int(size), transcendentals=0)


def whole(shape):
    zeros = (0,) * len(shape)
    return pl.BlockSpec(tuple(shape), lambda i, *_: zeros)


def swap(array, axis, size, bits):
    return lax.ppermute(array, axis, [(i, i ^ bits) for i in range(size)])


def rotate(wide, tables, sign):
    width = wide.shape[-1]
    half = ROT // 2
    lane = lax.broadcasted_iota(jnp.int32, (1, width), 1)
    turns = ((lane // HD) % 3 < 2).astype(F32)
    reps = width // tables.shape[-1]
    cosine, low, high = (jnp.concatenate([tables[j]] * reps, axis=1) * turns for j in range(3))
    down = pltpu.roll(wide, width - half, 1)
    up = pltpu.roll(wide, half, 1)
    return wide + wide * cosine + sign * (down * low + up * high)


EXCHANGE = (0, 2, 4, 6, 1, 3, 5, 7)
SMALL_ROWS = 16
SMALL_LANES = 128


def assemble_body(place, *refs, count, rows, small):
    blocks = refs[:count]
    full = refs[count]
    sems = refs[-1]
    copies = []
    for at, k in enumerate(EXCHANGE):
        start = pl.multiple_of((place[0] ^ k) * rows, 16)
        copies.append(
            pltpu.make_async_copy(
                blocks[at].at[pl.ds(0, rows), :], full.at[pl.ds(start, rows), :], sems.at[at]
            )
        )
        if small:
            copies.append(
                pltpu.make_async_copy(
                    blocks[at].at[pl.ds(rows, SMALL_ROWS), :], refs[-2].at[place[0] ^ k], sems.at[count + at]
                )
            )
    for copy in copies:
        copy.start()
    for copy in copies:
        copy.wait()
    if small:
        gains, qb, ub = refs[count + 1 : count + 4]
        nvec, heads, units = small
        lanes = SMALL_LANES
        qpart, upart = qb.shape[1] // heads // count, ub.shape[1] // units // count
        for d in range(count):
            wide = refs[-2][d].astype(F32)
            vals = wide[:, :lanes] + wide[:, lanes : 2 * lanes] + wide[:, 2 * lanes : 3 * lanes]
            gains[0:nvec, d * rows : (d + 1) * rows] = vals[0:nvec, :rows]
            for h in range(heads):
                at = (h * count + d) * qpart
                qb[:, at : at + qpart] = vals[nvec + h : nvec + h + 1, :qpart]
            for u in range(units):
                at = (u * count + d) * upart
                row = nvec + heads + u
                ub[:, at : at + upart] = vals[row : row + 1, :upart]


def assemble(place, blocks, rows, small):
    count = len(blocks)
    cols = blocks[0].shape[1]
    anywhere = pl.BlockSpec(memory_space=pl.ANY)
    outs = [jax.ShapeDtypeStruct((count * rows, cols), BF)]
    specs = [anywhere]
    scratch = []
    if small:
        nvec, qcols, heads, fcols, units = small
        outs += [
            jax.ShapeDtypeStruct(shape, F32) for shape in ((nvec, count * rows), (1, qcols), (1, fcols))
        ]
        specs += [whole(o.shape) for o in outs[1:]]
        scratch = [pltpu.VMEM((count, SMALL_ROWS, cols), BF)]
        small = (nvec, heads, units)
    return pl.pallas_call(
        functools.partial(assemble_body, count=count, rows=rows, small=small),
        grid_spec=pltpu.PrefetchScalarGridSpec(
            num_scalar_prefetch=1,
            grid=(1,),
            in_specs=[anywhere] * count,
            out_specs=specs,
            scratch_shapes=scratch + [pltpu.SemaphoreType.DMA((2 * count,))],
        ),
        out_shape=outs,
        compiler_params=vmem(4),
    )(place, *blocks)


def finish_body(meta, own, got_a, got_b, got_c, qkv_o, dense_o, qb_o, ub_o, stat_o, square, flat):
    qcols, acols = qkv_o.shape[1], dense_o.shape[0]
    rows = own.shape[0]
    total = own[...] + got_a[...].astype(F32) + got_b[...].astype(F32) + got_c[...].astype(F32)
    qkv_o[...] = total[:, :qcols]
    flat[...] = total[:, qcols:]
    square[...] = jnp.zeros_like(square)
    square[:rows, :] = flat[...]
    turned = square[...].T
    dense_o[...] = turned[:acols, :rows]
    stats = turned[acols : acols + 8, :]
    stat_o[...] = stats
    for out, row in ((qb_o, 7), (ub_o, 5)):
        groups, per = out.shape
        for g in range(groups):
            out[g : g + 1, :] = stats[row : row + 1, g * per : (g + 1) * per]


def prep_body(meta, cot, half_o, sum_o):
    half_o[...] = cot[...].astype(BF)
    sum_o[...] = jnp.broadcast_to(jnp.sum(cot[...], axis=0, keepdims=True), sum_o.shape)


def final_body(meta, own, one, two, hid, cot, out_o):
    x = hid[...].astype(F32)
    cent = x - jnp.mean(x, axis=-1, keepdims=True)
    inverse = lax.rsqrt(jnp.mean(cent * cent, axis=-1, keepdims=True) + norm_eps)
    normed = cent * inverse
    n = own[...].astype(F32) + one[...].astype(F32) + two[...].astype(F32)
    out_o[...] = cot[...] + inverse * (
        n - jnp.mean(n, axis=-1, keepdims=True) - normed * jnp.mean(n * normed, axis=-1, keepdims=True)
    )


def windows(length):
    reach = -(-(MAX_DOC - 1) // QB)
    return [(max(0, i - reach) * QB, (i + 1) * QB) for i in range(length // QB)]


def spot(meta, a, tokens):
    return pl.ds(pl.multiple_of(((meta[0] % 2) ^ a) * tokens, tokens), tokens)


def attn_fwd_body(
    meta, hid_a, hid_b, gains, wa, qb, tables, segc, segr,
    xhat_o, first_o, second_o, mixed_o, att_o, p_o, scratch,
):
    qcols = qb.shape[1]
    tokens = hid_a.shape[0]
    for a, hid in enumerate((hid_a, hid_b)):
        at = spot(meta, a, tokens)
        x = hid[...].astype(F32)
        cent = x - jnp.mean(x, axis=-1, keepdims=True)
        spread = jnp.mean(cent * cent, axis=-1, keepdims=True)
        xhat = cent * lax.rsqrt(spread + norm_eps)
        xhat_o[at, :] = xhat.astype(BF)
        first_o[at, :] = (xhat * gains[0:1, :] + gains[1:2, :]).astype(BF)
        second_o[at, :] = (xhat * gains[2:3, :] + gains[3:4, :]).astype(BF)
    seqs, _, length = segr.shape
    heads = qcols // (3 * HD)
    scratch[...] = jnp.zeros_like(scratch)
    for r in range(seqs):
        row = slice(r * length, (r + 1) * length)
        scratch[:, :qcols] = dot(first_o[row, :], wa[:, :qcols]) + qb[...]
        mixed_o[row, :] = rotate(scratch[...], tables, 1.0).astype(BF)
    for r in range(seqs):
        start = r * length
        for i, (lo, hi) in enumerate(windows(length)):
            width = hi - lo
            qs = slice(start + i * QB, start + (i + 1) * QB)
            ks = slice(start + lo, start + hi)
            rows = lax.broadcasted_iota(jnp.int32, (QB, width), 0) + i * QB
            cols = lax.broadcasted_iota(jnp.int32, (QB, width), 1) + lo
            mask = (segc[qs, :] == segr[r, :, lo:hi]) & (rows >= cols)
            for h in range(heads):
                base = h * 3 * HD
                q = mixed_o[qs, base : base + HD]
                k = mixed_o[ks, base + HD : base + 2 * HD]
                v = mixed_o[ks, base + 2 * HD : base + 3 * HD]
                s = jnp.where(mask, dot_t(q, k) * (HD**-0.5), -1e30)
                p = jnp.exp(s - jnp.max(s, axis=-1, keepdims=True))
                w = (p * (1.0 / jnp.sum(p, axis=-1, keepdims=True))).astype(BF)
                att_o[qs, h * HD : (h + 1) * HD] = dot(w, v).astype(BF)
                p_o[r, h, i, :, :width] = w


def mlp_fwd_body(meta, second, att, wa, wb, ub, active_o, slope_o, out_a, out_b, both, *, qcols):
    fcols = ub.shape[1]
    tokens = out_a.shape[0]

    @pl.loop(0, 2)
    def _(i):
        at = pl.ds(pl.multiple_of(i * tokens, tokens), tokens)
        pre = dot(second[at, :], wb[:, :fcols]) + ub[...]
        cumulative = 0.5 * (1.0 + lax.erf(pre * (1.0 / math.sqrt(2.0))))
        density = jnp.exp(-0.5 * pre * pre) * (1.0 / math.sqrt(2.0 * math.pi))
        act = (pre * cumulative).astype(BF)
        active_o[at, :] = act
        slope_o[at, :] = (cumulative + pre * density).astype(BF)
        both[at, :] = (dot_t(att[at, :], wa[:, qcols:]) + dot_t(act, wb[:, fcols:])).astype(BF)

    out_a[...] = both[spot(meta, 0, tokens), :]
    out_b[...] = both[spot(meta, 1, tokens), :]


def mlp_bwd_body(
    meta, cot_a, cot_b, act, slope, second, xhat, gains, wb, *refs, fcols, blocks, split, chained,
):
    tokens = cot_a.shape[0]
    if chained:
        up_in, down_in, ub_in, stat_in, n_o, keep_o, send_o, ub_o, stat_o, gup, gdown = refs
    else:
        n_o, gup, gdown, ub_o, stat_o = refs
    for a, ref in enumerate((cot_a, cot_b)):
        at = spot(meta, a, tokens)
        c = ref[...]
        down = t_dot(c, act[at, :])
        gp = dot(c, wb[:, fcols:]) * slope[at, :].astype(F32)
        gph = gp.astype(BF)
        up = t_dot(second[at, :], gph)
        part = dot_t(gph, wb[:, :fcols])
        n_o[at, :] = (part * gains[2:3, :]).astype(BF)
        sums = (
            jnp.sum(gp, axis=0, keepdims=True),
            jnp.sum(part * xhat[at, :].astype(F32), axis=0, keepdims=True),
            jnp.sum(part, axis=0, keepdims=True),
        )
        if a:
            gdown[...] += down
            gup[...] += up
            ub_o[0:1, :] += sums[0]
            stat_o[0:1, :] += sums[1]
            stat_o[1:2, :] += sums[2]
        elif chained:
            gdown[...] = down_in[...] + down
            gup[...] = up_in[...] + up
            ub_o[0:1, :] = ub_in[0:1, :] + sums[0]
            stat_o[0:1, :] = stat_in[0:1, :] + sums[1]
            stat_o[1:2, :] = stat_in[1:2, :] + sums[2]
        else:
            gdown[...] = down
            gup[...] = up
            ub_o[0:1, :] = sums[0]
            stat_o[0:1, :] = sums[1]
            stat_o[1:2, :] = sums[2]
    if chained:
        emit(meta, (gup, gdown), keep_o, send_o, blocks, split)


def emit(meta, parts, keep_o, send_o, blocks, split):
    rows = keep_o.shape[1]
    for k in range(blocks):
        if split:
            start = pl.multiple_of((meta[1] ^ k) * rows, 16)
            target = send_o if k % 2 else keep_o
            slot = k // 2
        else:
            start, target, slot = k * rows, keep_o, k
        at = 0
        for part in parts:
            wide = part.shape[1]
            target[slot, :, at : at + wide] = part[pl.ds(start, rows), :].astype(target.dtype)
            at += wide


def attn_bwd_body(
    meta, cot_a, cot_b, mix, p_in, att, first, xhat, n_in, gains, wa, tables,
    n_a, n_b, stat_o, qb_o, gqkv, gdense, dmix, cot, *, heads, qcols, seqs, last,
):
    tokens = cot_a.shape[0]
    for a, ref in enumerate((cot_a, cot_b)):
        cot[spot(meta, a, tokens), :] = ref[...]
    c = cot[...]
    length = c.shape[0] // seqs
    down = t_dot(c, att[...])
    gdense[...] = down if last is None else last[1][...] + down
    ga = dot(c, wa[:, qcols:]).astype(BF)
    dmix[...] = jnp.zeros_like(dmix)
    for r in range(seqs):
        start = r * length
        for h in range(heads):
            base = h * 3 * HD
            for i, (lo, hi) in enumerate(windows(length)):
                width = hi - lo
                qs = slice(start + i * QB, start + (i + 1) * QB)
                ks = slice(start + lo, start + hi)
                q = mix[qs, base : base + HD]
                k = mix[ks, base + HD : base + 2 * HD]
                v = mix[ks, base + 2 * HD : base + 3 * HD]
                g = ga[qs, h * HD : (h + 1) * HD]
                w = p_in[r, h, i, :, :width]
                wide = w.astype(F32)
                gw = dot_t(g, v)
                inner = jnp.sum(wide * gw, axis=-1, keepdims=True)
                ds = (wide * (gw - inner) * (HD**-0.5)).astype(BF)
                dmix[qs, base : base + HD] = dot(ds, k)
                dmix[ks, base + HD : base + 2 * HD] += t_dot(ds, q)
                dmix[ks, base + 2 * HD : base + 3 * HD] += t_dot(w, g)
        row = slice(start, start + length)
        dmix[row, :] = rotate(dmix[row, :], tables, -1.0)
    turned = dmix[...]
    total = jnp.sum(turned, axis=0, keepdims=True)
    qb_o[0:1, :] = total if last is None else last[3][0:1, :] + total
    g = turned[:, :qcols].astype(BF)
    up = t_dot(first[...], g)
    gqkv[...] = up if last is None else last[0][...] + up
    part = dot_t(g, wa[:, :qcols])
    sums = (
        jnp.sum(part * xhat[...].astype(F32), axis=0, keepdims=True),
        jnp.sum(part, axis=0, keepdims=True),
    )
    for j in range(2):
        stat_o[j : j + 1, :] = sums[j] if last is None else last[2][j : j + 1, :] + sums[j]
    cot[...] = (part * gains[0:1, :] + n_in[...].astype(F32)).astype(BF)
    for a, out in enumerate((n_a, n_b)):
        out[...] = cot[spot(meta, a, tokens), :]


def pack_body(
    meta, gqkv, gdense, stat, stat_two, cot_sum, ub, qb, keep_o, send_o, wide, cols,
    *, blocks, split, heads, units,
):
    rows = keep_o.shape[1]
    lanes = cols.shape[1]
    wide[...] = jnp.zeros_like(wide)
    wide[0:2, :] = stat[0:2, :]
    wide[2:4, :] = stat_two[0:2, :]
    wide[4:5, :] = cot_sum[0:1, :]
    cols[...] = wide[...].T
    for lane_at, source, groups, size in ((5, ub, units, ub.shape[1] // units), (7, qb, heads, 3 * HD)):
        per = size // blocks
        tall = jnp.broadcast_to(source[0:1, :], (lanes, source.shape[1])).T
        lane = lax.broadcasted_iota(jnp.int32, (per, lanes), 1)
        for d in range(blocks):
            for g in range(groups):
                at = slice(d * rows + g * per, d * rows + (g + 1) * per)
                src = tall[g * size + d * per : g * size + (d + 1) * per, :]
                cols[at, :] = jnp.where(lane == lane_at, src, cols[at, :])
    emit(meta, (gqkv, gdense, cols), keep_o, send_o, blocks, split)


def gather_weights(shard, rows, place, dp, small=None):
    got = {k: swap(shard, "dp", dp, k) for k in (6, 2, 4)}
    near = [shard] + [got[k] for k in (2, 4, 6)]
    far = [swap(a, "dp", dp, 1) for a in near]
    return assemble(place, near + far, rows, small)


def reduce_weights(keep, send, dp):
    if send is None:
        total = lax.psum_scatter(keep, "dp", scatter_dimension=0, tiled=True)[0]
        return [total] + [jnp.zeros_like(total)] * 3
    got = swap(send, "dp", dp, 1)
    near = [keep[j].astype(F32) + got[j].astype(F32) for j in range(keep.shape[0])]
    parts = [swap(near[j].astype(BF), "dp", dp, 2 * j) for j in (3, 1, 2)]
    return [near[0]] + parts


def rotary_tables(length):
    place = jnp.arange(length).astype(F32)[:, None]
    entry = jnp.arange(128) % HD
    half = ROT // 2
    turns = (entry < ROT)[None, :]
    frequency = 1.0 / 10000.0 ** ((entry % half).astype(F32) * 2.0 / ROT)
    angle = place * frequency[None, :]
    cosine = jnp.where(turns, jnp.cos(angle) - 1.0, 0.0)
    sine = jnp.where(turns, jnp.sin(angle), 0.0)
    low = (entry < half)[None, :]
    return jnp.stack([cosine, jnp.where(low, -sine, 0.0), jnp.where(low, 0.0, sine)])


def call(body, out_shape, scratch, *args, mib=16, flops=0):
    return pl.pallas_call(
        body,
        grid_spec=pltpu.PrefetchScalarGridSpec(
            num_scalar_prefetch=1,
            grid=(1,),
            in_specs=[whole(a.shape) for a in args[1:]],
            out_specs=[whole(o.shape) for o in out_shape],
            scratch_shapes=[pltpu.VMEM(shape, dtype) for shape, dtype in scratch],
        ),
        out_shape=out_shape,
        compiler_params=vmem(mib),
        cost_estimate=cost(flops, args[1:], out_shape),
    )(*args)


def block(
    hidden_in, segment_ids, cotangent, norm1_gain, norm1_bias, norm2_gain, norm2_bias,
    qkv_weight, qkv_bias, dense_weight, dense_bias, up_weight, up_bias, down_weight, down_bias,
    *, dp, tensor,
):
    d_at = lax.axis_index("dp")
    z_at = lax.axis_index("tensor")
    meta = jnp.stack([z_at, d_at]).astype(jnp.int32)
    place = d_at.astype(jnp.int32)[None]
    tokens, width = hidden_in.shape
    seqs, length = segment_ids.shape
    hseqs = seqs // 2
    htok = tokens * tensor // 2
    qcols = qkv_weight.shape[1]
    heads = qcols // (3 * HD)
    acols = heads * HD
    fcols = up_weight.shape[1]
    qwide = -(-qcols // 128) * 128
    rows = width // dp
    split = dp == len(EXCHANGE) and rows % 16 == 0
    stat_lanes = 128

    def sds(shape, dtype=F32):
        return jax.ShapeDtypeStruct(shape, dtype)

    def zswap(a, bits):
        return swap(a, "tensor", tensor, bits)

    vecs = jnp.stack([norm1_gain, norm1_bias, norm2_gain, norm2_bias, dense_bias, down_bias])
    nvec, part = vecs.shape
    got = [vecs] + [zswap(vecs, k) for k in range(1, tensor)]
    lanes_of = []
    for t in range(tensor):
        value = got[0]
        for k in range(1, tensor):
            value = jnp.where(z_at == t ^ k, got[k], value)
        lanes_of.append(value)
    units = up_bias.shape[0]

    def lanes(a):
        return jnp.pad(a.astype(F32), ((0, 0), (0, SMALL_LANES - a.shape[1])))

    small = jnp.concatenate(
        [
            lanes(jnp.concatenate(lanes_of, axis=1)), lanes(qkv_bias), lanes(up_bias),
            jnp.zeros((SMALL_ROWS - nvec - heads - units, SMALL_LANES), F32),
        ],
        axis=0,
    )
    high = lax.reduce_precision(small, 8, 7)
    middle = lax.reduce_precision(small - high, 8, 7)
    low = small - high - middle
    triple = jnp.concatenate([high, middle, low], axis=1).astype(BF)

    half_cot, cot_sum = call(
        prep_body, [sds((tokens, width), BF), sds((8, width))], [], meta, cotangent, mib=4
    )
    hid_two = zswap(hidden_in, 2)
    hid_one = zswap(hidden_in, 1)
    hid_three = zswap(hid_two, 1)
    cot_two = zswap(half_cot, 2)
    cot_one = zswap(half_cot, 1)
    cot_three = zswap(cot_two, 1)

    acols_all = qcols + acols
    triple = jnp.pad(triple, ((0, 0), (0, acols_all - triple.shape[1])))
    pack_a = jnp.concatenate(
        [jnp.concatenate([qkv_weight, dense_weight.T], axis=1), triple], axis=0
    )
    pack_b = jnp.concatenate([up_weight, down_weight.T], axis=1)
    if split:
        wa, gains, qb, ub = gather_weights(
            pack_a, rows, place, dp, (nvec, qcols, heads, fcols, units)
        )
        (wb,) = gather_weights(pack_b, rows, place, dp)
    else:
        every = lax.all_gather(pack_a, "dp", axis=0)
        wa = every[:, :rows].reshape(width, acols_all)
        wb = lax.all_gather(pack_b, "dp", axis=0, tiled=True)
        trio = every[:, rows:].astype(F32)
        vals = sum(trio[:, :, j * SMALL_LANES : (j + 1) * SMALL_LANES] for j in range(3))
        gains = vals[:, :nvec, :rows].transpose(1, 0, 2).reshape(nvec, width)
        qb = vals[:, nvec : nvec + heads, : 3 * HD // dp].transpose(1, 0, 2).reshape(1, qcols)
        ub = vals[:, nvec + heads : nvec + heads + units, : fcols // units // dp]
        ub = ub.transpose(1, 0, 2).reshape(1, fcols)
    tables = rotary_tables(length)

    side = z_at // 2
    near_ids = lax.dynamic_slice_in_dim(segment_ids, side * hseqs, hseqs, 0)
    far_ids = lax.dynamic_slice_in_dim(segment_ids, (1 - side) * hseqs, hseqs, 0)
    nwin = length // QB
    wwin = max(hi - lo for lo, hi in windows(length))

    def forward(hid_a, hid_b, ids):
        fa = call(
            attn_fwd_body,
            [
                sds((htok, width), BF), sds((htok, width), BF), sds((htok, width), BF),
                sds((htok, qwide), BF), sds((htok, acols), BF), sds((hseqs, heads, nwin, QB, wwin), BF),
            ],
            [((htok, qwide), F32)],
            meta, hid_a, hid_b, gains, wa, qb, tables, ids.reshape(htok, 1),
            ids.reshape(hseqs, 1, length), flops=7e9,
        )
        xhat, first, second, mixed, att, weights = fa
        active, slope, out_a, out_b = call(
            functools.partial(mlp_fwd_body, qcols=qcols),
            [
                sds((htok, fcols), BF), sds((htok, fcols), BF), sds((tokens, width), BF),
                sds((tokens, width), BF),
            ],
            [((htok, width), BF)], meta, second, att, wa, wb, ub, flops=3e9,
        )
        return dict(
            xhat=xhat, first=first, second=second, mixed=mixed, att=att, weights=weights,
            active=active, slope=slope, out=(out_a, out_b),
        )

    near = forward(hidden_in, hid_one, near_ids)
    far = forward(hid_two, hid_three, far_ids)

    def scatter(near_parts, far_parts):
        relay = zswap(far_parts[1], 1)
        pair = (far_parts[0].astype(F32) + relay.astype(F32)).astype(BF)
        two = zswap(pair, 2)
        one = zswap(near_parts[1], 1)
        return near_parts[0], one, two

    branch = sum(a.astype(F32) for a in scatter(near["out"], far["out"]))
    hidden_out = hidden_in.astype(F32) + branch + gains[4] + gains[5]

    if split:
        half_blocks = (dp // 2, rows)
    else:
        half_blocks = (dp, rows)

    def grad_shapes(cols):
        return [sds(half_blocks + (cols,)), sds(half_blocks + (cols,) if split else (1, 16, 128), BF)]

    def mlp_bwd(cot_a, cot_b, kept, before):
        sums = [sds((8, fcols)), sds((8, width))]
        grads = [sds((width, fcols)), sds((width, fcols))]
        chained = before is not None
        return call(
            functools.partial(mlp_bwd_body, fcols=fcols, blocks=dp, split=split, chained=chained),
            [sds((htok, width), BF)] + (grad_shapes(2 * fcols) + sums if chained else grads + sums),
            [((width, fcols), F32)] * 2 if chained else [],
            meta, cot_a, cot_b, *(kept[k] for k in ("active", "slope", "second", "xhat")), gains, wb,
            *(before if chained else ()), flops=5e9,
        )

    n_two_far, *sums_far = mlp_bwd(cot_two, cot_three, far, None)
    n_two_near, b_keep, b_send, ub_sum, stat_two = mlp_bwd(half_cot, cot_one, near, sums_far)

    def attn_bwd(cot_a, cot_b, kept, n_half, before):
        fixed = 12

        def body(*refs):
            ins = refs[:fixed]
            last = None if before is None else (refs[fixed], refs[fixed + 1], refs[fixed + 2], refs[fixed + 3])
            outs = refs[fixed + (0 if before is None else 4) :]
            attn_bwd_body(*ins, *outs, heads=heads, qcols=qcols, seqs=hseqs, last=last)

        return call(
            body,
            [
                sds((tokens, width), BF), sds((tokens, width), BF), sds((8, width)), sds((8, qwide)),
                sds((width, qcols)), sds((width, acols)),
            ],
            [((htok, qwide), F32), ((htok, width), BF)],
            meta, cot_a, cot_b, kept["mixed"], kept["weights"], kept["att"], kept["first"], kept["xhat"],
            n_half, gains, wa, tables, *(() if before is None else before), flops=9e9,
        )

    *n_far, s_far, q_far, gqkv_far, gdense_far = attn_bwd(cot_two, cot_three, far, n_two_far, None)
    *n_near, stat_one, qb_sum, gqkv, gdense = attn_bwd(
        half_cot, cot_one, near, n_two_near, (gqkv_far, gdense_far, s_far, q_far)
    )
    a_keep, a_send = call(
        functools.partial(pack_body, blocks=dp, split=split, heads=heads, units=units),
        grad_shapes(qcols + acols + stat_lanes),
        [((stat_lanes, width), F32), ((width, stat_lanes), F32)],
        meta, gqkv, gdense, stat_one, stat_two, cot_sum, ub_sum, qb_sum, flops=1e9,
    )

    b_grad = sum(a.astype(F32) for a in reduce_weights(b_keep, b_send if split else None, dp))
    grad_parts = scatter(n_near, n_far)
    lanes_up = -(-rows // 128) * 128
    qkv_grad, dense_grad, qb_grad, ub_grad, stats = call(
        finish_body,
        [
            sds((rows, qcols)), sds((acols, rows)), sds((heads, 3 * HD // dp)),
            sds((units, fcols // units // dp)), sds((8, lanes_up)),
        ],
        [((lanes_up, acols + stat_lanes), F32), ((rows, acols + stat_lanes), F32)],
        meta, *reduce_weights(a_keep, a_send if split else None, dp), mib=8, flops=1e9,
    )
    (hidden_grad,) = call(
        final_body, [sds((tokens, width))], [], meta, *grad_parts, hidden_in, cotangent, mib=8, flops=2e9
    )

    total = stats
    for k in range(1, tensor):
        total = total + zswap(stats, k)
    mine = lax.dynamic_slice_in_dim(total, z_at * part, part, 1)

    return (
        hidden_out,
        hidden_grad,
        mine[0],
        mine[1],
        mine[2],
        mine[3],
        qkv_grad,
        qb_grad,
        dense_grad,
        mine[4],
        b_grad[:, :fcols],
        ub_grad,
        b_grad[:, fcols:].T,
        mine[4],
    )


def solution(mesh):
    both = P(("dp", "tensor"))
    wide = P(("dp", "tensor"), None)
    step = jax.shard_map(
        functools.partial(block, dp=mesh.shape["dp"], tensor=mesh.shape["tensor"]),
        mesh=mesh,
        in_specs=(
            wide, P("dp", None), wide, both, both, both, both, P("dp", "tensor"),
            P("tensor", "dp"), P("tensor", "dp"), both, P("dp", "tensor"), P("tensor", "dp"),
            P("tensor", "dp"), both,
        ),
        out_specs=(
            wide, wide, both, both, both, both, P("dp", "tensor"), P("tensor", "dp"),
            P("tensor", "dp"), both, P("dp", "tensor"), P("tensor", "dp"), P("tensor", "dp"), both,
        ),
        check_vma=False,
    )
    if mesh.shape["dp"] != len(EXCHANGE):
        return step
    return step
```
